128 devices in a mesh: sub: 128 (over z, x, y, core).
Axes of the slice: x: 4, y: 4, z: 4, core: 2. Of those that a mesh axis runs over, the one named last changes fastest.
Arguments:
- inv_interior: bfloat16 [262144, 2048], P('sub'), may hold values from -0.125 to 0.125
- coupling: bfloat16 [262144, 512], P('sub'), may hold values from -0.29882812 to 0.29882812
- boundary: float32 [65536, 512], P('sub'), may hold values from -0.9 to 47
- residual: float32 [65536, 1024], P('sub'), may hold values from -15 to 15
- face_size: int32 [128, 4], P('sub'), may hold values from 64 to 128, as said below
- init_scale: float32 [128, 4], P('sub'), may hold values from 0.008 to 0.016, as said below
Outputs:
- schur: float32 [65536, 512], P('sub')
- averaged: float32 [65536, 1024], P('sub')
- inner: float32 [], replicated
The draws below stay inside these ranges and needn't reach their ends.
Inputs may be any that keep to these rules, and one draw needn't show every extreme that they name: `face_size`: both sharers of a face give it the same size; some face has 128 unknowns. `init_scale`: both sharers of a face give it the same scaling.
All inputs are finite; a program needn't handle non-finite values.
Results may differ from the reference program's by a relative error of at most 0.0003.
Values sent between devices are 32-bit elements; how exact they have to be, the bound alone decides.
A program may use at most 64 MiB of HBM per device.

```python
import jax
import jax.numpy as jnp
from jax import lax

NI = 2048
NB = 512
NF = 4
FMAX = 128
COLS = 1024
NS_STEPS = 4
SUBS = 128


def shared_rows(key):
    owners = jnp.arange(SUBS, dtype=jnp.int32)[:, None]
    powers = jnp.array([SUBS // 2 ** (face + 1) for face in range(NF)], dtype=jnp.int32)[None, :]
    return (owners - jnp.bitwise_and(owners, powers)).astype(jnp.int32)


def draw_face_size(key, part):
    shared = shared_rows(key)
    table = jax.random.randint(jax.random.fold_in(key, 12), (SUBS, NF), FMAX // 2, FMAX + 1).astype(jnp.int32)
    table = table.at[0, :].set(FMAX).at[2, 0].set(FMAX // 2)
    return table[shared, jnp.arange(NF)[None, :]].astype(jnp.int32)


def draw_init_scale(key, part):
    shared = shared_rows(key)
    lower = jnp.log(0.008)
    upper = jnp.log(0.016)
    table = jnp.exp(jax.random.uniform(jax.random.fold_in(key, 13), (SUBS, NF), jnp.float32, lower, upper))
    return table[shared, jnp.arange(NF)[None, :]].astype(jnp.float32)


def draw_boundary(key, part):
    diag = 6.0 + jnp.exp(jax.random.uniform(jax.random.fold_in(key, 14), (SUBS, NB), jnp.float32, 0.0, jnp.log(40.0)))
    spread = jnp.clip(0.15 * jax.random.normal(jax.random.fold_in(key, 15), (SUBS, NB, NB), jnp.float32), -0.9, 0.9)
    ident = jnp.eye(NB, dtype=jnp.float32)
    full = spread * (1.0 - ident)[None] + diag[:, :, None] * ident[None]
    return full.reshape(SUBS * NB, NB).astype(jnp.float32)


def draw_residual(key, part):
    values = jnp.clip(jax.random.normal(jax.random.fold_in(key, 16), (SUBS, NB, COLS), jnp.float32), -5.0, 5.0)
    rising = 1.0 + 2.0 * jnp.arange(SUBS, dtype=jnp.float32) / (SUBS - 1)
    return (values * rising[:, None, None]).reshape(SUBS * NB, COLS).astype(jnp.float32)


def shard_levels(key, shape, cuts, low, largest):
    gain, own = 1.0, jax.random.fold_in(key, 6)
    for dim, parts in cuts:
        heights = jnp.exp(jax.random.uniform(jax.random.fold_in(own, dim), (parts,), jnp.float32, low / len(cuts), largest / len(cuts)))
        gain = gain * jnp.repeat(heights, shape[dim] // parts).reshape([-1 if axis == dim else 1 for axis in range(len(shape))])
    return gain


def gaussian(rng, extent, scale, reach, split=(), held_as=jnp.bfloat16):
    level = shard_levels(rng, extent, split, -0.22, 0.18) if split else 1.0
    entries = jax.random.normal(rng, extent, jnp.float32) * scale * level
    return jnp.minimum(jnp.maximum(entries, -reach), reach).astype(held_as)


def setup_inputs(seed: int = 0) -> dict:
    splits = jax.random.split(jax.random.key(seed), 7)
    return {
        "inv_interior": gaussian(splits[0], (SUBS * NI, NI), NI ** -0.5, 0.125, ((0, 128),)),
        "coupling": gaussian(splits[1], (SUBS * NI, NB), 0.05, 0.29882812, ((0, 128),)),
        "boundary": draw_boundary(jax.random.fold_in(splits[6], 71), 0),
        "residual": draw_residual(jax.random.fold_in(splits[6], 71), 0),
        "face_size": draw_face_size(jax.random.fold_in(splits[6], 71), 0),
        "init_scale": draw_init_scale(jax.random.fold_in(splits[6], 71), 0),
    }


def condense(inv, cpl, bnd):
    solved = jnp.dot(inv, cpl, preferred_element_type=jnp.float32).astype(jnp.bfloat16)
    return bnd - jnp.dot(cpl.T, solved, preferred_element_type=jnp.float32)


def face_parts(schur, resid, sizes):
    starts = jnp.concatenate([jnp.zeros((1,), jnp.int32), jnp.cumsum(sizes).astype(jnp.int32)[:-1]]).astype(jnp.int32)
    lanes = jnp.arange(FMAX, dtype=jnp.int32)
    valid = (lanes[None, :] < sizes[:, None]).astype(schur.dtype)
    blocks = []
    pieces = []
    for face in range(NF):
        start = starts[face]
        block = lax.dynamic_slice(schur, (start, start), (FMAX, FMAX))
        piece = lax.dynamic_slice(resid, (start, jnp.int32(0)), (FMAX, COLS))
        blocks.append(block * valid[face][:, None] * valid[face][None, :])
        pieces.append(piece * valid[face][:, None])
    return jnp.stack(blocks), jnp.stack(pieces), valid, starts


def place(resid, face_avg, valid, starts):
    result = resid
    for face in range(NF):
        start = starts[face]
        current = lax.dynamic_slice(result, (start, jnp.int32(0)), (FMAX, COLS))
        fresh = jnp.where(valid[face][:, None] > 0, face_avg[face], current)
        result = lax.dynamic_update_slice(result, fresh, (start, jnp.int32(0)))
    return result


def reference(inv_interior, coupling, boundary, residual, face_size, init_scale):
    inv = inv_interior.reshape(SUBS, NI, NI)
    cpl = coupling.reshape(SUBS, NI, NB)
    bnd = boundary.reshape(SUBS, NB, NB)
    resid = residual.reshape(SUBS, NB, COLS)
    schur = lax.map(lambda item: condense(item[0], item[1], item[2]), (inv, cpl, bnd))
    blocks, pieces, valid, starts = jax.vmap(face_parts)(schur, resid, face_size)
    owners = jnp.arange(SUBS, dtype=jnp.int32)[:, None]
    powers = jnp.array([SUBS // (2 ** (face + 1)) for face in range(NF)], dtype=jnp.int32)[None, :]
    mates = jnp.bitwise_xor(owners, powers).astype(jnp.int32)
    faces = jnp.arange(NF, dtype=jnp.int32)[None, :]
    other_block = blocks[mates, faces]
    other_piece = pieces[mates, faces]
    total = blocks + other_block
    ident = jnp.eye(FMAX, dtype=total.dtype)
    approx = init_scale[:, :, None, None] * ident[None, None] * valid[:, :, None, :]
    high = lax.Precision.HIGHEST
    for step in range(NS_STEPS):
        product = jnp.einsum("dfij,dfjk->dfik", total, approx, precision=high)
        approx = 2.0 * approx - jnp.einsum("dfij,dfjk->dfik", approx, product, precision=high)
    weight_own = jnp.einsum("dfij,dfjk->dfik", approx, blocks, precision=high)
    weight_other = jnp.einsum("dfij,dfjk->dfik", approx, other_block, precision=high)
    face_avg = jnp.einsum("dfij,dfjk->dfik", weight_own, pieces, precision=high) + jnp.einsum("dfij,dfjk->dfik", weight_other, other_piece, precision=high)
    averaged = jax.vmap(place)(resid, face_avg, valid, starts)
    inner = jnp.sum(resid * averaged)
    return schur.reshape(SUBS * NB, NB), averaged.reshape(SUBS * NB, COLS), inner
```

```python
import functools

import jax
import jax.numpy as jnp
from jax import lax
from jax.experimental import pallas as pl
from jax.experimental.pallas import tpu as pltpu
from jax.sharding import PartitionSpec as P

FMAX = 128
STEPS = 4
CHUNKS = 4
EARLY = 2
MROWS = 512
SPAN = FMAX + 8
MESH = pl.DeviceIdType.MESH


def flip(me, mask):
    return me + mask - 2 * mask * ((me // mask) % 2)


def flips(me, masks, which):
    for bit, mask in enumerate(masks):
        if (which >> bit) & 1:
            me = flip(me, mask)
    return me


def rank(me, masks):
    total = 0
    for bit, mask in enumerate(masks):
        total = total + ((me // mask) % 2) * (1 << bit)
    return total


def halves(x):
    hi = x.astype(jnp.bfloat16)
    lo = (x - hi.astype(jnp.float32)).astype(jnp.bfloat16)
    return hi, lo


def mm(a, b):
    return jnp.dot(a, b, preferred_element_type=jnp.float32)


def square_product(a, b):
    ah, al = halves(a)
    bh, bl = halves(b)
    row = jnp.concatenate([bh, bl], axis=1)
    both = mm(jnp.concatenate([ah, al], axis=1), jnp.concatenate([row, row], axis=0))
    return both[:, :FMAX] + both[:, FMAX:]


def turned(x, shift):
    amount = jnp.full((1, 8, x.shape[2]), shift, jnp.int32)
    for bit in (1, 2, 4):
        x = jnp.where((amount & bit) != 0, jnp.roll(x, bit, axis=1), x)
    return x


def rows_at(ref, start, columns):
    base = jnp.minimum(lax.div(start, 8), (ref.shape[0] - FMAX) // 8 - 1) * 8
    shift = start - base
    x = ref[pl.ds(base, FMAX + 8), columns]
    w = x.shape[1]
    x = turned(x.reshape(FMAX // 8 + 1, 8, w), 8 - shift)
    row = lax.broadcasted_iota(jnp.int32, (1, 8, w), 1)
    return jnp.where(row < 8 - shift, x[:-1], x[1:]).reshape(FMAX, w)


def rows_down(x, shift):
    w = x.shape[1]
    pad = jnp.zeros((1, 8, w), x.dtype)
    x = jnp.concatenate([pad, x.reshape(FMAX // 8, 8, w), pad], axis=0)
    x = turned(x, shift)
    row = lax.broadcasted_iota(jnp.int32, (1, 8, w), 1)
    return jnp.where(row < shift, x[:-1], x[1:]).reshape(FMAX + 8, w)


def kernel(
    masks,
    groups,
    inv_hbm,
    cpl_hbm,
    bnd_hbm,
    res_hbm,
    size_ref,
    scale_ref,
    schur_ref,
    avg_ref,
    inner_ref,
    inv,
    cpl,
    sol,
    bnd,
    res,
    own,
    oth,
    own_b,
    oth_b,
    face,
    wbuf,
    red,
    in_sem,
    inv_sem,
    s_sem,
    r_sem,
    sb_sem,
    rb_sem,
    sr_sem,
    rr_sem,
):
    me = lax.axis_index("sub")
    faces = len(masks)
    ni, nb = cpl.shape
    columns = res.shape[1]
    width = columns // CHUNKS

    load_res = pltpu.make_async_copy(res_hbm, res, in_sem.at[0])
    load_res.start()
    load_cpl = pltpu.make_async_copy(cpl_hbm, cpl, in_sem.at[1])
    load_cpl.start()
    load_inv = [
        pltpu.make_async_copy(
            inv_hbm.at[pl.ds(i * MROWS, MROWS)], inv.at[pl.ds(i * MROWS, MROWS)], inv_sem.at[i]
        )
        for i in range(ni // MROWS)
    ]
    for copy in load_inv:
        copy.start()
    load_bnd = pltpu.make_async_copy(bnd_hbm, bnd, in_sem.at[2])
    load_bnd.start()

    mates = [flip(me, mask) for mask in masks]
    peers = []
    for group in groups:
        peers += [flips(me, group, which) for which in range(1, 1 << len(group))]
    barrier = pltpu.get_barrier_semaphore()
    for peer in peers:
        pl.semaphore_signal(barrier, inc=1, device_id=(peer,), device_id_type=MESH)

    odd = 0
    for mask in masks:
        odd = odd + (me // mask) % 2
    odd = odd % 2
    sizes = [size_ref[0, r] for r in range(faces)]
    starts = [jnp.int32(0)]
    for r in range(faces):
        starts.append(starts[-1] + sizes[r])
    whole = [lax.div(start, 8) * 8 for start in starts]
    face[...] = jnp.zeros_like(face)

    load_res.wait()
    rows = lax.broadcasted_iota(jnp.int32, (FMAX, width), 0)
    for k in range(CHUNKS):
        c = (1 - odd) * k + odd * (CHUNKS - 1 - k)
        at = pl.multiple_of(c * width, width)
        for r in range(faces):
            piece = rows_at(res, starts[r], pl.ds(at, width))
            own[k, r] = jnp.where(rows < sizes[r], piece, 0.0)

    pl.semaphore_wait(barrier, len(peers))
    copies = [
        [
            pltpu.make_async_remote_copy(
                src_ref=own.at[k, r],
                dst_ref=oth.at[k, r],
                send_sem=s_sem.at[k, r],
                recv_sem=r_sem.at[k, r],
                device_id=(mates[r],),
                device_id_type=MESH,
            )
            for r in range(faces)
        ]
        for k in range(CHUNKS)
    ]
    for k in range(EARLY):
        for r in range(faces):
            copies[k][r].start()

    load_cpl.wait()
    for i in range(ni // MROWS):
        load_inv[i].wait()
        sol[pl.ds(i * MROWS, MROWS), :] = mm(inv[pl.ds(i * MROWS, MROWS), :], cpl[...]).astype(
            jnp.bfloat16
        )
    load_bnd.wait()
    schur_ref[...] = bnd[...] - lax.dot_general(
        cpl[...], sol[...], (((0,), (0,)), ((), ())), preferred_element_type=jnp.float32
    )

    i0 = lax.broadcasted_iota(jnp.int32, (FMAX, FMAX), 0)
    i1 = lax.broadcasted_iota(jnp.int32, (FMAX, FMAX), 1)
    for r in range(faces):
        left = jnp.minimum(lax.div(starts[r], FMAX), nb // FMAX - 2) * FMAX
        band = rows_at(schur_ref, starts[r], pl.ds(left, 2 * FMAX))
        b0 = lax.broadcasted_iota(jnp.int32, (2 * FMAX, FMAX), 0)
        b1 = lax.broadcasted_iota(jnp.int32, (2 * FMAX, FMAX), 1)
        pick = jnp.where(b0 == b1 + (starts[r] - left), 1.0, 0.0).astype(jnp.bfloat16)
        hi, lo = halves(band)
        rest = band - hi.astype(jnp.float32) - lo.astype(jnp.float32)
        parts = mm(jnp.concatenate([hi, lo, rest.astype(jnp.bfloat16)], axis=0), pick)
        block = parts[:FMAX] + parts[FMAX : 2 * FMAX] + parts[2 * FMAX :]
        own_b[r] = jnp.where((i0 < sizes[r]) & (i1 < sizes[r]), block, 0.0)
    block_copies = [
        pltpu.make_async_remote_copy(
            src_ref=own_b.at[r],
            dst_ref=oth_b.at[r],
            send_sem=sb_sem.at[r],
            recv_sem=rb_sem.at[r],
            device_id=(mates[r],),
            device_id_type=MESH,
        )
        for r in range(faces)
    ]
    for copy in block_copies:
        copy.start()
    for k in range(EARLY, CHUNKS):
        for r in range(faces):
            copies[k][r].start()

    es, xs = [], []
    for r in range(faces):
        block_copies[r].wait_recv()
        scale = scale_ref[0, r]
        ident = jnp.where((i0 == i1) & (i0 < sizes[r]), 1.0, 0.0)
        e = ident - scale * (own_b[r] + oth_b[r])
        xs.append(scale * (ident + e))
        es.append(e)
    for step in range(1, STEPS):
        es = [square_product(e, e) for e in es]
        xs = [x + square_product(x, e) for x, e in zip(xs, es)]
    for r in range(faces):
        w = jnp.concatenate(
            [square_product(xs[r], own_b[r]), square_product(xs[r], oth_b[r])], axis=1
        )
        wh, wl = halves(w)
        wbuf[r, pl.ds(0, FMAX), :] = wh
        wbuf[r, pl.ds(FMAX, FMAX), :] = wl

    def fold(x):
        total = None
        for a in range(0, x.shape[0], 8):
            for b in range(0, x.shape[1], 128):
                t = x[a : a + 8, b : b + 128]
                total = t if total is None else total + t
        return total

    row8 = lax.broadcasted_iota(jnp.int32, (8, 128), 0)
    partial = jnp.zeros((8, 128), jnp.float32)
    low = faces * (FMAX // 2)
    for a in range(low, nb, 8):
        t = res[pl.ds(a, 8), :]
        t = fold(t * t)
        partial = partial + jnp.where(row8 + a >= starts[faces], t, 0.0)

    for k in range(CHUNKS):
        c = odd * k + (1 - odd) * (CHUNKS - 1 - k)
        at = pl.multiple_of(c * width, width)
        for r in range(faces):
            copies[k][r].wait_recv()
            mine, theirs = own[CHUNKS - 1 - k, r], oth[k, r]
            ph, pw = halves(jnp.concatenate([mine, theirs], axis=0))
            top = mm(wbuf[r], ph)
            value = top[:FMAX] + top[FMAX:] + mm(wbuf[r, pl.ds(0, FMAX), :], pw)
            face[pl.ds(r * SPAN, SPAN), :] = rows_down(value, starts[r] - whole[r])
            if k < CHUNKS // 2:
                partial = partial + fold((mine + theirs) * value)
        for a in range(0, nb, 8):
            t = res[pl.ds(a, 8), pl.ds(at, width)]
            here = lax.broadcasted_iota(jnp.int32, (8, width), 0) + a
            for r in range(faces):
                if a >= r * (FMAX // 2) and a < (r + 1) * FMAX:
                    tile = a // 8 + r * (SPAN // 8) - lax.div(starts[r], 8)
                    tile = jnp.clip(tile, 0, face.shape[0] // 8 - 1)
                    shifted = face[pl.ds(tile * 8, 8), :]
                    t = jnp.where((here >= starts[r]) & (here < starts[r + 1]), shifted, t)
            avg_ref[pl.ds(a, 8), pl.ds(at, width)] = t

    base = 0
    sends = []
    for g, group in enumerate(groups):
        mine = rank(me, group)
        red[base + mine] = partial
        n = 1 << len(group)
        round_copies = []
        for which in range(1, n):
            round_copies.append(
                pltpu.make_async_remote_copy(
                    src_ref=red.at[base + mine],
                    dst_ref=red.at[base + mine],
                    send_sem=sr_sem.at[base + which],
                    recv_sem=rr_sem.at[base + which],
                    device_id=(flips(me, group, which),),
                    device_id_type=MESH,
                )
            )
        for copy in round_copies:
            copy.start()
        for copy in round_copies:
            copy.wait_recv()
        sends += round_copies
        partial = red[base]
        for j in range(1, n):
            partial = partial + red[base + j]
        base += n
    inner_ref[0, 0] = jnp.sum(partial)

    for copy in sends:
        copy.wait_send()
    for copy in block_copies:
        copy.wait_send()
    for row in copies:
        for copy in row:
            copy.wait_send()


def local(inv_interior, coupling, boundary, residual, face_size, init_scale):
    ni, nb = coupling.shape
    columns = residual.shape[1]
    faces = face_size.shape[1]
    subs = lax.axis_size("sub")
    masks = [subs >> (r + 1) for r in range(faces)]
    groups = [[1, 2, 4], [8, 16], [32, 64]]
    slots = sum(1 << len(g) for g in groups)
    width = columns // CHUNKS
    f32, bf16 = jnp.float32, jnp.bfloat16
    anyspec = pl.BlockSpec(memory_space=pl.ANY)
    smem = pl.BlockSpec(memory_space=pltpu.SMEM)
    vmem = pl.BlockSpec(memory_space=pltpu.VMEM)
    dma = pltpu.SemaphoreType.DMA
    schur, averaged, inner = pl.pallas_call(
        functools.partial(kernel, masks, groups),
        name="deluxe",
        out_shape=(
            jax.ShapeDtypeStruct((nb, nb), f32),
            jax.ShapeDtypeStruct((nb, columns), f32),
            jax.ShapeDtypeStruct((1, 1), f32),
        ),
        in_specs=[anyspec, anyspec, anyspec, anyspec, smem, smem],
        out_specs=(vmem, vmem, smem),
        scratch_shapes=[
            pltpu.VMEM((ni, ni), bf16),
            pltpu.VMEM((ni, nb), bf16),
            pltpu.VMEM((ni, nb), bf16),
            pltpu.VMEM((nb, nb), f32),
            pltpu.VMEM((nb, columns), f32),
            pltpu.VMEM((CHUNKS, faces, FMAX, width), f32),
            pltpu.VMEM((CHUNKS, faces, FMAX, width), f32),
            pltpu.VMEM((faces, FMAX, FMAX), f32),
            pltpu.VMEM((faces, FMAX, FMAX), f32),
            pltpu.VMEM((faces * SPAN + (faces - 1) * (FMAX // 2) - 8, width), f32),
            pltpu.VMEM((faces, 2 * FMAX, 2 * FMAX), bf16),
            pltpu.VMEM((slots, 8, 128), f32),
            dma((3,)),
            dma((ni // MROWS,)),
            dma((CHUNKS, faces)),
            dma((CHUNKS, faces)),
            dma((faces,)),
            dma((faces,)),
            dma((slots,)),
            dma((slots,)),
        ],
        compiler_params=pltpu.CompilerParams(
            collective_id=0, has_side_effects=True, vmem_limit_bytes=56 * 2**20
        ),
    )(inv_interior, coupling, boundary, residual, face_size, init_scale)
    return (schur, averaged, inner[0, 0])


def solution(mesh):
    spec = P("sub", None)
    return jax.shard_map(
        local,
        mesh=mesh,
        in_specs=(spec,) * 6,
        out_specs=(spec, spec, P()),
        check_vma=False,
    )
```

```python
import functools

import jax
import jax.numpy as jnp
from jax import lax
from jax.experimental import pallas as pl
from jax.experimental.pallas import tpu as pltpu
from jax.sharding import PartitionSpec as P

FMAX = 128
STEPS = 4
CHUNKS = 8
EARLY = 3
HALF = CHUNKS // 2
MROWS = 512
SPAN = FMAX + 8
MESH = pl.DeviceIdType.MESH


def flip(me, mask):
    return me + mask - 2 * mask * ((me // mask) % 2)


def flips(me, masks, which):
    for bit, mask in enumerate(masks):
        if (which >> bit) & 1:
            me = flip(me, mask)
    return me


def rank(me, masks):
    total = 0
    for bit, mask in enumerate(masks):
        total = total + ((me // mask) % 2) * (1 << bit)
    return total


def halves(x):
    hi = x.astype(jnp.bfloat16)
    lo = (x - hi.astype(jnp.float32)).astype(jnp.bfloat16)
    return hi, lo


def mm(a, b):
    return jnp.dot(a, b, preferred_element_type=jnp.float32)


def square_product(a, b):
    ah, al = halves(a)
    bh, bl = halves(b)
    row = jnp.concatenate([bh, bl], axis=1)
    both = mm(jnp.concatenate([ah, al], axis=1), jnp.concatenate([row, row], axis=0))
    return both[:, :FMAX] + both[:, FMAX:]


def turned(x, shift):
    amount = jnp.full((1, 8, x.shape[2]), shift, jnp.int32)
    for bit in (1, 2, 4):
        x = jnp.where((amount & bit) != 0, jnp.roll(x, bit, axis=1), x)
    return x


def rows_at(ref, start, columns):
    base = jnp.minimum(lax.div(start, 8), (ref.shape[0] - FMAX) // 8 - 1) * 8
    shift = start - base
    x = ref[pl.ds(base, FMAX + 8), columns]
    w = x.shape[1]
    x = turned(x.reshape(FMAX // 8 + 1, 8, w), 8 - shift)
    row = lax.broadcasted_iota(jnp.int32, (1, 8, w), 1)
    return jnp.where(row < 8 - shift, x[:-1], x[1:]).reshape(FMAX, w)


def rows_down(x, shift):
    w = x.shape[1]
    pad = jnp.zeros((1, 8, w), x.dtype)
    x = jnp.concatenate([pad, x.reshape(FMAX // 8, 8, w), pad], axis=0)
    x = turned(x, shift)
    row = lax.broadcasted_iota(jnp.int32, (1, 8, w), 1)
    return jnp.where(row < shift, x[:-1], x[1:]).reshape(FMAX + 8, w)


def kernel(
    masks,
    groups,
    inv_hbm,
    cpl_hbm,
    bnd_hbm,
    res_hbm,
    size_ref,
    scale_ref,
    schur_ref,
    avg_ref,
    inner_ref,
    inv,
    cpl,
    sol,
    bnd,
    res,
    own,
    oth,
    own_b,
    oth_b,
    face,
    wbuf,
    red,
    in_sem,
    inv_sem,
    s_sem,
    r_sem,
    sb_sem,
    rb_sem,
    sr_sem,
    rr_sem,
):
    me = lax.axis_index("sub")
    faces = len(masks)
    ni, nb = cpl.shape
    columns = res.shape[1]
    width = columns // CHUNKS

    load_res = pltpu.make_async_copy(res_hbm, res, in_sem.at[0])
    load_res.start()
    mates = [flip(me, mask) for mask in masks]
    peers = []
    for group in groups:
        peers += [flips(me, group, which) for which in range(1, 1 << len(group))]
    barrier = pltpu.get_barrier_semaphore()
    for peer in peers:
        pl.semaphore_signal(barrier, inc=1, device_id=(peer,), device_id_type=MESH)

    odd = 0
    for mask in masks:
        odd = odd + (me // mask) % 2
    odd = odd % 2
    sizes = [size_ref[0, r] for r in range(faces)]
    starts = [jnp.int32(0)]
    for r in range(faces):
        starts.append(starts[-1] + sizes[r])
    whole = [lax.div(start, 8) * 8 for start in starts]
    face[...] = jnp.zeros_like(face)

    load_res.wait()
    load_cpl = pltpu.make_async_copy(cpl_hbm, cpl, in_sem.at[1])
    load_cpl.start()
    load_inv = [
        pltpu.make_async_copy(
            inv_hbm.at[pl.ds(i * MROWS, MROWS)], inv.at[pl.ds(i * MROWS, MROWS)], inv_sem.at[i]
        )
        for i in range(ni // MROWS)
    ]
    for copy in load_inv:
        copy.start()
    load_bnd = pltpu.make_async_copy(bnd_hbm, bnd, in_sem.at[2])
    load_bnd.start()

    copies = [
        [
            pltpu.make_async_remote_copy(
                src_ref=own.at[k, r],
                dst_ref=oth.at[k, r],
                send_sem=s_sem.at[k, r],
                recv_sem=r_sem.at[k, r],
                device_id=(mates[r],),
                device_id_type=MESH,
            )
            for r in range(faces)
        ]
        for k in range(CHUNKS)
    ]

    def issue(k):
        for r in range(faces):
            copies[k][r].start()

    rows = lax.broadcasted_iota(jnp.int32, (FMAX, width), 0)
    for k in range(CHUNKS):
        c = (1 - odd) * k + odd * (CHUNKS - 1 - k)
        at = pl.multiple_of(c * width, width)
        for r in range(faces):
            piece = rows_at(res, starts[r], pl.ds(at, width))
            own[k, r] = jnp.where(rows < sizes[r], piece, 0.0)
        if k == 1:
            pl.semaphore_wait(barrier, len(peers))
        if 1 <= k <= EARLY:
            issue(k - 1)

    load_cpl.wait()
    for i in range(ni // MROWS):
        load_inv[i].wait()
        sol[pl.ds(i * MROWS, MROWS), :] = mm(inv[pl.ds(i * MROWS, MROWS), :], cpl[...]).astype(
            jnp.bfloat16
        )
    load_bnd.wait()
    schur_ref[...] = bnd[...] - lax.dot_general(
        cpl[...], sol[...], (((0,), (0,)), ((), ())), preferred_element_type=jnp.float32
    )

    i0 = lax.broadcasted_iota(jnp.int32, (FMAX, FMAX), 0)
    i1 = lax.broadcasted_iota(jnp.int32, (FMAX, FMAX), 1)
    for r in range(faces):
        left = jnp.minimum(lax.div(starts[r], FMAX), nb // FMAX - 2) * FMAX
        band = rows_at(schur_ref, starts[r], pl.ds(left, 2 * FMAX))
        b0 = lax.broadcasted_iota(jnp.int32, (2 * FMAX, FMAX), 0)
        b1 = lax.broadcasted_iota(jnp.int32, (2 * FMAX, FMAX), 1)
        pick = jnp.where(b0 == b1 + (starts[r] - left), 1.0, 0.0).astype(jnp.bfloat16)
        hi, lo = halves(band)
        rest = band - hi.astype(jnp.float32) - lo.astype(jnp.float32)
        parts = mm(jnp.concatenate([hi, lo, rest.astype(jnp.bfloat16)], axis=0), pick)
        block = parts[:FMAX] + parts[FMAX : 2 * FMAX] + parts[2 * FMAX :]
        own_b[r] = jnp.where((i0 < sizes[r]) & (i1 < sizes[r]), block, 0.0)
    block_copies = [
        pltpu.make_async_remote_copy(
            src_ref=own_b.at[r],
            dst_ref=oth_b.at[r],
            send_sem=sb_sem.at[r],
            recv_sem=rb_sem.at[r],
            device_id=(mates[r],),
            device_id_type=MESH,
        )
        for r in range(faces)
    ]
    for copy in block_copies:
        copy.start()
    for k in range(EARLY, HALF + 2):
        issue(k)

    es, xs = [], []
    for r in range(faces):
        block_copies[r].wait_recv()
        scale = scale_ref[0, r]
        ident = jnp.where((i0 == i1) & (i0 < sizes[r]), 1.0, 0.0)
        e = ident - scale * (own_b[r] + oth_b[r])
        xs.append(scale * (ident + e))
        es.append(e)
    for step in range(1, STEPS):
        es = [square_product(e, e) for e in es]
        xs = [x + square_product(x, e) for x, e in zip(xs, es)]
    for r in range(faces):
        w = jnp.concatenate(
            [square_product(xs[r], own_b[r]), square_product(xs[r], oth_b[r])], axis=1
        )
        wh, wl = halves(w)
        wbuf[r, pl.ds(0, FMAX), :] = wh
        wbuf[r, pl.ds(FMAX, FMAX), :] = wl

    def fold(x):
        total = None
        for a in range(0, x.shape[0], 8):
            for b in range(0, x.shape[1], 128):
                t = x[a : a + 8, b : b + 128]
                total = t if total is None else total + t
        return total

    row8 = lax.broadcasted_iota(jnp.int32, (8, 128), 0)
    partial = jnp.zeros((8, 128), jnp.float32)
    low = faces * (FMAX // 2)
    for a in range(low, nb, 8):
        t = res[pl.ds(a, 8), :]
        t = fold(t * t)
        partial = partial + jnp.where(row8 + a >= starts[faces], t, 0.0)

    def finish(ks):
        pair = jnp.zeros((8, 128), jnp.float32)
        values = []
        for r in range(faces):
            for k in ks:
                copies[k][r].wait_recv()
            both = [jnp.concatenate([own[CHUNKS - 1 - k, r], oth[k, r]], axis=0) for k in ks]
            ph, pw = halves(jnp.concatenate(both, axis=1))
            top = mm(wbuf[r], ph)
            value = top[:FMAX] + top[FMAX:] + mm(wbuf[r, pl.ds(0, FMAX), :], pw)
            values.append(value)
            for j, k in enumerate(ks):
                if k < HALF:
                    part = value[:, j * width : (j + 1) * width]
                    pair = pair + fold((both[j][:FMAX] + both[j][FMAX:]) * part)
        for j, k in enumerate(ks):
            c = odd * k + (1 - odd) * (CHUNKS - 1 - k)
            at = pl.multiple_of(c * width, width)
            for r in range(faces):
                part = values[r][:, j * width : (j + 1) * width]
                face[k % 2, pl.ds(r * SPAN, SPAN), :] = rows_down(part, starts[r] - whole[r])
            here = lax.broadcasted_iota(jnp.int32, (8, width), 0)
            for a in range(0, nb, 8):
                t = res[pl.ds(a, 8), pl.ds(at, width)]
                for r in range(faces):
                    if a >= r * (FMAX // 2) and a < (r + 1) * FMAX:
                        tile = a // 8 + r * (SPAN // 8) - lax.div(starts[r], 8)
                        tile = jnp.clip(tile, 0, face.shape[1] // 8 - 1)
                        shifted = face[k % 2, pl.ds(tile * 8, 8), :]
                        t = jnp.where(
                            (here >= starts[r] - a) & (here < starts[r + 1] - a), shifted, t
                        )
                avg_ref[pl.ds(a, 8), pl.ds(at, width)] = t
        return pair

    bases = [0]
    for group in groups:
        bases.append(bases[-1] + (1 << len(group)))

    def spread(g, value):
        mine = bases[g] + rank(me, groups[g])
        red[mine] = value
        round_copies = [
            pltpu.make_async_remote_copy(
                src_ref=red.at[mine],
                dst_ref=red.at[mine],
                send_sem=sr_sem.at[bases[g] + which],
                recv_sem=rr_sem.at[bases[g] + which],
                device_id=(flips(me, groups[g], which),),
                device_id_type=MESH,
            )
            for which in range(1, 1 << len(groups[g]))
        ]
        for copy in round_copies:
            copy.start()
        return round_copies

    def gather(g, round_copies):
        for copy in round_copies:
            copy.wait_recv()
        total = red[bases[g]]
        for j in range(bases[g] + 1, bases[g + 1]):
            total = total + red[j]
        return total

    for k in range(0, HALF, 2):
        partial = partial + finish((k, k + 1))
    sends = []
    for g in range(len(groups)):
        round_copies = spread(g, partial)
        sends += round_copies
        if HALF + 2 + g < CHUNKS:
            issue(HALF + 2 + g)
        finish((HALF + g,))
        partial = gather(g, round_copies)
    for k in range(HALF + len(groups), CHUNKS):
        finish((k,))
    inner_ref[0, 0] = jnp.sum(partial)

    for copy in sends:
        copy.wait_send()
    for copy in block_copies:
        copy.wait_send()
    for row in copies:
        for copy in row:
            copy.wait_send()


def local(inv_interior, coupling, boundary, residual, face_size, init_scale):
    ni, nb = coupling.shape
    columns = residual.shape[1]
    faces = face_size.shape[1]
    subs = lax.axis_size("sub")
    masks = [subs >> (r + 1) for r in range(faces)]
    groups = [[8, 16], [32, 64], [1, 2, 4]]
    slots = sum(1 << len(g) for g in groups)
    width = columns // CHUNKS
    f32, bf16 = jnp.float32, jnp.bfloat16
    anyspec = pl.BlockSpec(memory_space=pl.ANY)
    smem = pl.BlockSpec(memory_space=pltpu.SMEM)
    vmem = pl.BlockSpec(memory_space=pltpu.VMEM)
    dma = pltpu.SemaphoreType.DMA
    schur, averaged, inner = pl.pallas_call(
        functools.partial(kernel, masks, groups),
        name="deluxe",
        out_shape=(
            pltpu.VMEM((nb, nb), f32),
            pltpu.VMEM((nb, columns), f32),
            jax.ShapeDtypeStruct((1, 1), f32),
        ),
        in_specs=[anyspec, anyspec, anyspec, anyspec, smem, smem],
        out_specs=(vmem, vmem, smem),
        scratch_shapes=[
            pltpu.VMEM((ni, ni), bf16),
            pltpu.VMEM((ni, nb), bf16),
            pltpu.VMEM((ni, nb), bf16),
            pltpu.VMEM((nb, nb), f32),
            pltpu.VMEM((nb, columns), f32),
            pltpu.VMEM((CHUNKS, faces, FMAX, width), f32),
            pltpu.VMEM((CHUNKS, faces, FMAX, width), f32),
            pltpu.VMEM((faces, FMAX, FMAX), f32),
            pltpu.VMEM((faces, FMAX, FMAX), f32),
            pltpu.VMEM((2, faces * SPAN + (faces - 1) * (FMAX // 2) - 8, width), f32),
            pltpu.VMEM((faces, 2 * FMAX, 2 * FMAX), bf16),
            pltpu.VMEM((slots, 8, 128), f32),
            dma((3,)),
            dma((ni // MROWS,)),
            dma((CHUNKS, faces)),
            dma((CHUNKS, faces)),
            dma((faces,)),
            dma((faces,)),
            dma((slots,)),
            dma((slots,)),
        ],
        compiler_params=pltpu.CompilerParams(
            collective_id=0, has_side_effects=True, vmem_limit_bytes=56 * 2**20
        ),
    )(inv_interior, coupling, boundary, residual, face_size, init_scale)
    return (schur, averaged, inner[0, 0])


def solution(mesh):
    spec = P("sub", None)
    return jax.shard_map(
        local,
        mesh=mesh,
        in_specs=(spec,) * 6,
        out_specs=(spec, spec, P()),
        check_vma=False,
    )
```

```python
import functools

import jax
import jax.numpy as jnp
from jax import lax
from jax.experimental import pallas as pl
from jax.experimental.pallas import tpu as pltpu
from jax.sharding import PartitionSpec as P

FMAX = 128
STEPS = 4
CHUNKS = 8
EARLY = 3
HALF = CHUNKS // 2
MROWS = 512
SPAN = FMAX + 8
MESH = pl.DeviceIdType.MESH


def flip(me, mask):
    return me + mask - 2 * mask * ((me // mask) % 2)


def flips(me, masks, which):
    for bit, mask in enumerate(masks):
        if (which >> bit) & 1:
            me = flip(me, mask)
    return me


def rank(me, masks):
    total = 0
    for bit, mask in enumerate(masks):
        total = total + ((me // mask) % 2) * (1 << bit)
    return total


def halves(x):
    hi = x.astype(jnp.bfloat16)
    lo = (x - hi.astype(jnp.float32)).astype(jnp.bfloat16)
    return hi, lo


def mm(a, b):
    return jnp.dot(a, b, preferred_element_type=jnp.float32)


def square_product(a, b):
    ah, al = halves(a)
    bh, bl = halves(b)
    row = jnp.concatenate([bh, bl], axis=1)
    both = mm(jnp.concatenate([ah, al], axis=1), jnp.concatenate([row, row], axis=0))
    return both[:, :FMAX] + both[:, FMAX:]


def turned(x, shift):
    amount = jnp.full((1, 8, x.shape[2]), shift, jnp.int32)
    for bit in (1, 2, 4):
        x = jnp.where((amount & bit) != 0, jnp.roll(x, bit, axis=1), x)
    return x


def rows_at(ref, start, columns):
    base = jnp.minimum(lax.div(start, 8), (ref.shape[0] - FMAX) // 8 - 1) * 8
    shift = start - base
    x = ref[pl.ds(base, FMAX + 8), columns]
    w = x.shape[1]
    x = turned(x.reshape(FMAX // 8 + 1, 8, w), 8 - shift)
    row = lax.broadcasted_iota(jnp.int32, (1, 8, w), 1)
    return jnp.where(row < 8 - shift, x[:-1], x[1:]).reshape(FMAX, w)


def rows_down(x, shift):
    w = x.shape[1]
    pad = jnp.zeros((1, 8, w), x.dtype)
    x = jnp.concatenate([pad, x.reshape(FMAX // 8, 8, w), pad], axis=0)
    x = turned(x, shift)
    row = lax.broadcasted_iota(jnp.int32, (1, 8, w), 1)
    return jnp.where(row < shift, x[:-1], x[1:]).reshape(FMAX + 8, w)


def kernel(
    masks,
    groups,
    inv_hbm,
    cpl_hbm,
    bnd_hbm,
    res_hbm,
    size_ref,
    scale_ref,
    schur_ref,
    avg_ref,
    inner_ref,
    inv,
    cpl,
    sol,
    bnd,
    res,
    own,
    oth,
    own_b,
    oth_b,
    face,
    wbuf,
    red,
    in_sem,
    inv_sem,
    s_sem,
    r_sem,
    sb_sem,
    rb_sem,
    sr_sem,
    rr_sem,
):
    me = lax.axis_index("sub")
    faces = len(masks)
    ni, nb = cpl.shape
    columns = res.shape[1]
    width = columns // CHUNKS

    load_res = pltpu.make_async_copy(res_hbm, res, in_sem.at[0])
    load_res.start()
    mates = [flip(me, mask) for mask in masks]
    peers = []
    for group in groups:
        peers += [flips(me, group, which) for which in range(1, 1 << len(group))]
    barrier = pltpu.get_barrier_semaphore()
    for peer in peers:
        pl.semaphore_signal(barrier, inc=1, device_id=(peer,), device_id_type=MESH)

    odd = 0
    for mask in masks:
        odd = odd + (me // mask) % 2
    odd = odd % 2
    sizes = [size_ref[0, r] for r in range(faces)]
    starts = [jnp.int32(0)]
    for r in range(faces):
        starts.append(starts[-1] + sizes[r])
    whole = [lax.div(start, 8) * 8 for start in starts]
    face[...] = jnp.zeros_like(face)

    load_res.wait()
    load_cpl = pltpu.make_async_copy(cpl_hbm, cpl, in_sem.at[1])
    load_cpl.start()
    load_inv = [
        pltpu.make_async_copy(
            inv_hbm.at[pl.ds(i * MROWS, MROWS)], inv.at[pl.ds(i * MROWS, MROWS)], inv_sem.at[i]
        )
        for i in range(ni // MROWS)
    ]
    for copy in load_inv:
        copy.start()
    load_bnd = pltpu.make_async_copy(bnd_hbm, bnd, in_sem.at[2])
    load_bnd.start()

    copies = [
        [
            pltpu.make_async_remote_copy(
                src_ref=own.at[k, r],
                dst_ref=oth.at[k, r],
                send_sem=s_sem.at[k, r],
                recv_sem=r_sem.at[k, r],
                device_id=(mates[r],),
                device_id_type=MESH,
            )
            for r in range(faces)
        ]
        for k in range(CHUNKS)
    ]

    def issue(k):
        for r in range(faces):
            copies[k][r].start()

    rows = lax.broadcasted_iota(jnp.int32, (FMAX, width), 0)

    def extract(k):
        c = (1 - odd) * k + odd * (CHUNKS - 1 - k)
        at = pl.multiple_of(c * width, width)
        for r in range(faces):
            piece = rows_at(res, starts[r], pl.ds(at, width))
            own[k, r] = jnp.where(rows < sizes[r], piece, 0.0)

    extract(0)
    extract(1)
    pl.semaphore_wait(barrier, len(peers))
    issue(0)
    load_cpl.wait()
    steps = ni // MROWS
    for i in range(steps):
        load_inv[i].wait()
        if i + 2 < CHUNKS:
            extract(i + 2)
        sol[pl.ds(i * MROWS, MROWS), :] = mm(inv[pl.ds(i * MROWS, MROWS), :], cpl[...]).astype(
            jnp.bfloat16
        )
        if i + 1 < EARLY:
            issue(i + 1)
    for k in range(steps + 2, CHUNKS):
        extract(k)
    load_bnd.wait()
    schur_ref[...] = bnd[...] - lax.dot_general(
        cpl[...], sol[...], (((0,), (0,)), ((), ())), preferred_element_type=jnp.float32
    )

    i0 = lax.broadcasted_iota(jnp.int32, (FMAX, FMAX), 0)
    i1 = lax.broadcasted_iota(jnp.int32, (FMAX, FMAX), 1)
    for r in range(faces):
        left = jnp.minimum(lax.div(starts[r], FMAX), nb // FMAX - 2) * FMAX
        band = rows_at(schur_ref, starts[r], pl.ds(left, 2 * FMAX))
        b0 = lax.broadcasted_iota(jnp.int32, (2 * FMAX, FMAX), 0)
        b1 = lax.broadcasted_iota(jnp.int32, (2 * FMAX, FMAX), 1)
        pick = jnp.where(b0 == b1 + (starts[r] - left), 1.0, 0.0).astype(jnp.bfloat16)
        hi, lo = halves(band)
        rest = band - hi.astype(jnp.float32) - lo.astype(jnp.float32)
        parts = mm(jnp.concatenate([hi, lo, rest.astype(jnp.bfloat16)], axis=0), pick)
        block = parts[:FMAX] + parts[FMAX : 2 * FMAX] + parts[2 * FMAX :]
        own_b[r] = jnp.where((i0 < sizes[r]) & (i1 < sizes[r]), block, 0.0)
    block_copies = [
        pltpu.make_async_remote_copy(
            src_ref=own_b.at[r],
            dst_ref=oth_b.at[r],
            send_sem=sb_sem.at[r],
            recv_sem=rb_sem.at[r],
            device_id=(mates[r],),
            device_id_type=MESH,
        )
        for r in range(faces)
    ]
    for copy in block_copies:
        copy.start()
    for k in range(EARLY, HALF + 2):
        issue(k)

    es, xs = [], []
    for r in range(faces):
        block_copies[r].wait_recv()
        scale = scale_ref[0, r]
        ident = jnp.where((i0 == i1) & (i0 < sizes[r]), 1.0, 0.0)
        e = ident - scale * (own_b[r] + oth_b[r])
        xs.append(scale * (ident + e))
        es.append(e)
    for step in range(1, STEPS):
        es = [square_product(e, e) for e in es]
        xs = [x + square_product(x, e) for x, e in zip(xs, es)]
    for r in range(faces):
        w = jnp.concatenate(
            [square_product(xs[r], own_b[r]), square_product(xs[r], oth_b[r])], axis=1
        )
        wh, wl = halves(w)
        wbuf[r, pl.ds(0, FMAX), :] = wh
        wbuf[r, pl.ds(FMAX, FMAX), :] = wl

    def fold(x):
        total = None
        for a in range(0, x.shape[0], 8):
            for b in range(0, x.shape[1], 128):
                t = x[a : a + 8, b : b + 128]
                total = t if total is None else total + t
        return total

    row8 = lax.broadcasted_iota(jnp.int32, (8, 128), 0)
    partial = jnp.zeros((8, 128), jnp.float32)
    low = faces * (FMAX // 2)
    for a in range(low, nb, 8):
        t = res[pl.ds(a, 8), :]
        t = fold(t * t)
        partial = partial + jnp.where(row8 + a >= starts[faces], t, 0.0)

    def finish(ks):
        pair = jnp.zeros((8, 128), jnp.float32)
        values = []
        for r in range(faces):
            for k in ks:
                copies[k][r].wait_recv()
            both = [jnp.concatenate([own[CHUNKS - 1 - k, r], oth[k, r]], axis=0) for k in ks]
            ph, pw = halves(jnp.concatenate(both, axis=1))
            top = mm(wbuf[r], ph)
            value = top[:FMAX] + top[FMAX:] + mm(wbuf[r, pl.ds(0, FMAX), :], pw)
            values.append(value)
            for j, k in enumerate(ks):
                if k < HALF:
                    part = value[:, j * width : (j + 1) * width]
                    pair = pair + fold((both[j][:FMAX] + both[j][FMAX:]) * part)
        for j, k in enumerate(ks):
            c = odd * k + (1 - odd) * (CHUNKS - 1 - k)
            at = pl.multiple_of(c * width, width)
            for r in range(faces):
                part = values[r][:, j * width : (j + 1) * width]
                face[k % 2, pl.ds(r * SPAN, SPAN), :] = rows_down(part, starts[r] - whole[r])
            here = lax.broadcasted_iota(jnp.int32, (8, width), 0)
            for a in range(0, nb, 8):
                t = res[pl.ds(a, 8), pl.ds(at, width)]
                for r in range(faces):
                    if a >= r * (FMAX // 2) and a < (r + 1) * FMAX:
                        tile = a // 8 + r * (SPAN // 8) - lax.div(starts[r], 8)
                        tile = jnp.clip(tile, 0, face.shape[1] // 8 - 1)
                        shifted = face[k % 2, pl.ds(tile * 8, 8), :]
                        t = jnp.where(
                            (here >= starts[r] - a) & (here < starts[r + 1] - a), shifted, t
                        )
                avg_ref[pl.ds(a, 8), pl.ds(at, width)] = t
        return pair

    bases = [0]
    for group in groups:
        bases.append(bases[-1] + (1 << len(group)))

    def spread(g, value):
        mine = bases[g] + rank(me, groups[g])
        red[mine] = value
        round_copies = [
            pltpu.make_async_remote_copy(
                src_ref=red.at[mine],
                dst_ref=red.at[mine],
                send_sem=sr_sem.at[bases[g] + which],
                recv_sem=rr_sem.at[bases[g] + which],
                device_id=(flips(me, groups[g], which),),
                device_id_type=MESH,
            )
            for which in range(1, 1 << len(groups[g]))
        ]
        for copy in round_copies:
            copy.start()
        return round_copies

    def gather(g, round_copies):
        for copy in round_copies:
            copy.wait_recv()
        total = red[bases[g]]
        for j in range(bases[g] + 1, bases[g + 1]):
            total = total + red[j]
        return total

    for k in range(0, HALF, 2):
        partial = partial + finish((k, k + 1))
    partial = jnp.sum(partial, axis=0, keepdims=True)
    sends = []
    for g in range(len(groups)):
        round_copies = spread(g, partial)
        sends += round_copies
        if HALF + 2 + g < CHUNKS:
            issue(HALF + 2 + g)
        finish((HALF + g,))
        partial = gather(g, round_copies)
    for k in range(HALF + len(groups), CHUNKS):
        finish((k,))
    inner_ref[0, 0] = jnp.sum(partial)

    for copy in sends:
        copy.wait_send()
    for copy in block_copies:
        copy.wait_send()
    for row in copies:
        for copy in row:
            copy.wait_send()


def copy_out(schur_ref, avg_ref, inner_ref, schur_out, avg_out, inner_out, sem):
    copies = [
        pltpu.make_async_copy(avg_ref, avg_out, sem.at[0]),
        pltpu.make_async_copy(schur_ref, schur_out, sem.at[1]),
    ]
    for copy in copies:
        copy.start()
    inner_out[0, 0] = inner_ref[0, 0]
    for copy in copies:
        copy.wait()


def local(inv_interior, coupling, boundary, residual, face_size, init_scale):
    ni, nb = coupling.shape
    columns = residual.shape[1]
    faces = face_size.shape[1]
    subs = lax.axis_size("sub")
    masks = [subs >> (r + 1) for r in range(faces)]
    groups = [[1, 2, 4], [8, 16, 32, 64]]
    slots = sum(1 << len(g) for g in groups)
    width = columns // CHUNKS
    f32, bf16 = jnp.float32, jnp.bfloat16
    anyspec = pl.BlockSpec(memory_space=pl.ANY)
    smem = pl.BlockSpec(memory_space=pltpu.SMEM)
    vmem = pl.BlockSpec(memory_space=pltpu.VMEM)
    dma = pltpu.SemaphoreType.DMA
    schur, averaged, inner = pl.pallas_call(
        functools.partial(kernel, masks, groups),
        name="deluxe",
        out_shape=(
            pltpu.VMEM((nb, nb), f32),
            pltpu.VMEM((nb, columns), f32),
            pltpu.SMEM((1, 1), f32),
        ),
        in_specs=[anyspec, anyspec, anyspec, anyspec, smem, smem],
        out_specs=(vmem, vmem, smem),
        scratch_shapes=[
            pltpu.VMEM((ni, ni), bf16),
            pltpu.VMEM((ni, nb), bf16),
            pltpu.VMEM((ni, nb), bf16),
            pltpu.VMEM((nb, nb), f32),
            pltpu.VMEM((nb, columns), f32),
            pltpu.VMEM((CHUNKS, faces, FMAX, width), f32),
            pltpu.VMEM((CHUNKS, faces, FMAX, width), f32),
            pltpu.VMEM((faces, FMAX, FMAX), f32),
            pltpu.VMEM((faces, FMAX, FMAX), f32),
            pltpu.VMEM((2, faces * SPAN + (faces - 1) * (FMAX // 2) - 8, width), f32),
            pltpu.VMEM((faces, 2 * FMAX, 2 * FMAX), bf16),
            pltpu.VMEM((slots, 1, 128), f32),
            dma((3,)),
            dma((ni // MROWS,)),
            dma((CHUNKS, faces)),
            dma((CHUNKS, faces)),
            dma((faces,)),
            dma((faces,)),
            dma((slots,)),
            dma((slots,)),
        ],
        compiler_params=pltpu.CompilerParams(
            collective_id=0, has_side_effects=True, vmem_limit_bytes=56 * 2**20
        ),
    )(inv_interior, coupling, boundary, residual, face_size, init_scale)
    schur, averaged, inner = pl.pallas_call(
        copy_out,
        name="copy_out",
        out_shape=(
            jax.ShapeDtypeStruct((nb, nb), f32),
            jax.ShapeDtypeStruct((nb, columns), f32),
            jax.ShapeDtypeStruct((1, 1), f32),
        ),
        in_specs=[vmem, vmem, smem],
        out_specs=(anyspec, anyspec, smem),
        scratch_shapes=[dma((2,))],
    )(
        pltpu.with_memory_space_constraint(schur, pltpu.VMEM),
        pltpu.with_memory_space_constraint(averaged, pltpu.VMEM),
        pltpu.with_memory_space_constraint(inner, pltpu.SMEM),
    )
    return (schur, averaged, inner[0, 0])


def solution(mesh):
    spec = P("sub", None)
    return jax.shard_map(
        local,
        mesh=mesh,
        in_specs=(spec,) * 6,
        out_specs=(spec, spec, P()),
        check_vma=False,
    )
```

```python
import functools

import jax
import jax.numpy as jnp
from jax import lax
from jax.experimental import pallas as pl
from jax.experimental.pallas import tpu as pltpu
from jax.sharding import PartitionSpec as P

FMAX = 128
STEPS = 4
CHUNKS = 8
EARLY = 3
HALF = CHUNKS // 2
MROWS = 512
SPAN = FMAX + 8
MESH = pl.DeviceIdType.MESH


def flip(me, mask):
    return me + mask - 2 * mask * ((me // mask) % 2)


def flips(me, masks, which):
    for bit, mask in enumerate(masks):
        if (which >> bit) & 1:
            me = flip(me, mask)
    return me


def rank(me, masks):
    total = 0
    for bit, mask in enumerate(masks):
        total = total + ((me // mask) % 2) * (1 << bit)
    return total


def halves(x):
    hi = x.astype(jnp.bfloat16)
    lo = (x - hi.astype(jnp.float32)).astype(jnp.bfloat16)
    return hi, lo


def mm(a, b):
    return jnp.dot(a, b, preferred_element_type=jnp.float32)


def square_product(a, b):
    ah, al = halves(a)
    bh, bl = halves(b)
    row = jnp.concatenate([bh, bl], axis=1)
    both = mm(jnp.concatenate([ah, al], axis=1), jnp.concatenate([row, row], axis=0))
    return both[:, :FMAX] + both[:, FMAX:]


def turned(x, shift):
    amount = jnp.full((1, 8, x.shape[2]), shift, jnp.int32)
    for bit in (1, 2, 4):
        x = jnp.where((amount & bit) != 0, jnp.roll(x, bit, axis=1), x)
    return x


def rows_at(ref, start, columns):
    base = jnp.minimum(lax.div(start, 8), (ref.shape[0] - FMAX) // 8 - 1) * 8
    shift = start - base
    x = ref[pl.ds(base, FMAX + 8), columns]
    w = x.shape[1]
    x = turned(x.reshape(FMAX // 8 + 1, 8, w), 8 - shift)
    row = lax.broadcasted_iota(jnp.int32, (1, 8, w), 1)
    return jnp.where(row < 8 - shift, x[:-1], x[1:]).reshape(FMAX, w)


def rows_down(x, shift):
    w = x.shape[1]
    pad = jnp.zeros((1, 8, w), x.dtype)
    x = jnp.concatenate([pad, x.reshape(FMAX // 8, 8, w), pad], axis=0)
    x = turned(x, shift)
    row = lax.broadcasted_iota(jnp.int32, (1, 8, w), 1)
    return jnp.where(row < shift, x[:-1], x[1:]).reshape(FMAX + 8, w)


def kernel(
    masks,
    groups,
    inv_hbm,
    cpl_hbm,
    bnd_hbm,
    res_hbm,
    size_ref,
    scale_ref,
    schur_ref,
    avg_ref,
    inner_ref,
    inv,
    cpl,
    sol,
    bnd,
    res,
    own,
    oth,
    own_b,
    oth_b,
    val,
    face,
    wbuf,
    red,
    in_sem,
    inv_sem,
    s_sem,
    r_sem,
    sb_sem,
    rb_sem,
    sr_sem,
    rr_sem,
    hello_sem,
):
    me = lax.axis_index("sub")
    faces = len(masks)
    ni, nb = cpl.shape
    columns = res.shape[1]
    width = columns // CHUNKS

    load_res = pltpu.make_async_copy(res_hbm, res, in_sem.at[0])
    load_res.start()
    mates = [flip(me, mask) for mask in masks]
    peers = [flip(me, mask) for group in groups for mask in group]
    barrier = pltpu.get_barrier_semaphore()
    for peer in peers:
        pl.semaphore_signal(barrier, inc=1, device_id=(peer,), device_id_type=MESH)

    odd = 0
    for mask in masks:
        odd = odd + (me // mask) % 2
    odd = odd % 2
    sizes = [size_ref[0, r] for r in range(faces)]
    starts = [jnp.int32(0)]
    for r in range(faces):
        starts.append(starts[-1] + sizes[r])
    whole = [lax.div(start, 8) * 8 for start in starts]
    face[...] = jnp.zeros_like(face)

    load_res.wait()
    load_cpl = pltpu.make_async_copy(cpl_hbm, cpl, in_sem.at[1])
    load_cpl.start()
    load_inv = [
        pltpu.make_async_copy(
            inv_hbm.at[pl.ds(i * MROWS, MROWS)], inv.at[pl.ds(i * MROWS, MROWS)], inv_sem.at[i]
        )
        for i in range(ni // MROWS)
    ]
    for copy in load_inv:
        copy.start()
    load_bnd = pltpu.make_async_copy(bnd_hbm, bnd, in_sem.at[2])
    load_bnd.start()

    copies = [
        [
            pltpu.make_async_remote_copy(
                src_ref=own.at[k, r],
                dst_ref=oth.at[k, r],
                send_sem=s_sem.at[k, r],
                recv_sem=r_sem.at[k, r],
                device_id=(mates[r],),
                device_id_type=MESH,
            )
            for r in range(faces)
        ]
        for k in range(CHUNKS)
    ]

    def issue(k, part=0):
        for r in range(faces):
            if part == 0 or r % 2 == part - 1:
                copies[k][r].start()

    rows = lax.broadcasted_iota(jnp.int32, (FMAX, width), 0)

    def greet(stage):
        for peer in peers:
            pl.semaphore_signal(
                hello_sem.at[stage], inc=1, device_id=(peer,), device_id_type=MESH
            )

    def greeted(stage):
        pl.semaphore_wait(hello_sem.at[stage], len(peers))

    def column(k):
        return pl.multiple_of(((1 - odd) * k + odd * (CHUNKS - 1 - k)) * width, width)

    def extract(k):
        for r in range(faces):
            piece = rows_at(res, starts[r], pl.ds(column(k), width))
            own[k, r] = jnp.where(rows < sizes[r], piece, 0.0)

    extract(0)
    extract(1)
    pl.semaphore_wait(barrier, len(peers))
    issue(0)
    greet(0)
    load_cpl.wait()
    steps = ni // MROWS
    for i in range(steps):
        load_inv[i].wait()
        if i + 2 < CHUNKS:
            extract(i + 2)
        sol[pl.ds(i * MROWS, MROWS), :] = mm(inv[pl.ds(i * MROWS, MROWS), :], cpl[...]).astype(
            jnp.bfloat16
        )
        if i + 1 < EARLY:
            issue(i + 1)
    for k in range(steps + 2, CHUNKS):
        extract(k)
    greeted(0)
    greet(1)
    load_bnd.wait()
    schur_ref[...] = bnd[...] - lax.dot_general(
        cpl[...], sol[...], (((0,), (0,)), ((), ())), preferred_element_type=jnp.float32
    )

    i0 = lax.broadcasted_iota(jnp.int32, (FMAX, FMAX), 0)
    i1 = lax.broadcasted_iota(jnp.int32, (FMAX, FMAX), 1)
    for r in range(faces):
        left = jnp.minimum(lax.div(starts[r], FMAX), nb // FMAX - 2) * FMAX
        band = rows_at(schur_ref, starts[r], pl.ds(left, 2 * FMAX))
        b0 = lax.broadcasted_iota(jnp.int32, (2 * FMAX, FMAX), 0)
        b1 = lax.broadcasted_iota(jnp.int32, (2 * FMAX, FMAX), 1)
        pick = jnp.where(b0 == b1 + (starts[r] - left), 1.0, 0.0).astype(jnp.bfloat16)
        hi, lo = halves(band)
        rest = band - hi.astype(jnp.float32) - lo.astype(jnp.float32)
        parts = mm(jnp.concatenate([hi, lo, rest.astype(jnp.bfloat16)], axis=0), pick)
        block = parts[:FMAX] + parts[FMAX : 2 * FMAX] + parts[2 * FMAX :]
        own_b[r] = jnp.where((i0 < sizes[r]) & (i1 < sizes[r]), block, 0.0)
    block_copies = [
        pltpu.make_async_remote_copy(
            src_ref=own_b.at[r],
            dst_ref=oth_b.at[r],
            send_sem=sb_sem.at[r],
            recv_sem=rb_sem.at[r],
            device_id=(mates[r],),
            device_id_type=MESH,
        )
        for r in range(faces)
    ]
    for copy in block_copies:
        copy.start()
    for k in range(EARLY, HALF + 2):
        issue(k)
    greeted(1)
    greet(2)

    es, xs = [], []
    for r in range(faces):
        block_copies[r].wait_recv()
        scale = scale_ref[0, r]
        ident = jnp.where((i0 == i1) & (i0 < sizes[r]), 1.0, 0.0)
        e = ident - scale * (own_b[r] + oth_b[r])
        xs.append(scale * (ident + e))
        es.append(e)
    for step in range(1, STEPS):
        es = [square_product(e, e) for e in es]
        xs = [x + square_product(x, e) for x, e in zip(xs, es)]
    for r in range(faces):
        w = jnp.concatenate(
            [square_product(xs[r], own_b[r]), square_product(xs[r], oth_b[r])], axis=1
        )
        wh, wl = halves(w)
        wbuf[r, pl.ds(0, FMAX), :] = wh
        wbuf[r, pl.ds(FMAX, FMAX), :] = wl

    def fold(x):
        total = None
        for a in range(0, x.shape[0], 8):
            for b in range(0, x.shape[1], 128):
                t = x[a : a + 8, b : b + 128]
                total = t if total is None else total + t
        return total

    row8 = lax.broadcasted_iota(jnp.int32, (8, 128), 0)
    partial = jnp.zeros((8, 128), jnp.float32)
    low = faces * (FMAX // 2)
    for a in range(low, nb, 8):
        t = res[pl.ds(a, 8), :]
        t = fold(t * t)
        partial = partial + jnp.where(row8 + a >= starts[faces], t, 0.0)

    def average(ks):
        pair = jnp.zeros((8, 128), jnp.float32)
        for r in range(faces):
            for k in ks:
                copies[k][r].wait_recv()
            both = [jnp.concatenate([own[CHUNKS - 1 - k, r], oth[k, r]], axis=0) for k in ks]
            ph, pw = halves(jnp.concatenate(both, axis=1))
            top = mm(wbuf[r], ph)
            value = top[:FMAX] + top[FMAX:] + mm(wbuf[r, pl.ds(0, FMAX), :], pw)
            for j, k in enumerate(ks):
                part = value[:, j * width : (j + 1) * width]
                val[k, r] = part
                if k < HALF:
                    pair = pair + fold((both[j][:FMAX] + both[j][FMAX:]) * part)
        return pair

    def place(k):
        at = column(CHUNKS - 1 - k)
        for r in range(faces):
            face[k % 2, pl.ds(r * SPAN, SPAN), :] = rows_down(val[k, r], starts[r] - whole[r])
        here = lax.broadcasted_iota(jnp.int32, (8, width), 0)
        for a in range(0, nb, 8):
            t = res[pl.ds(a, 8), pl.ds(at, width)]
            for r in range(faces):
                if a >= r * (FMAX // 2) and a < (r + 1) * FMAX:
                    tile = a // 8 + r * (SPAN // 8) - lax.div(starts[r], 8)
                    tile = jnp.clip(tile, 0, face.shape[1] // 8 - 1)
                    shifted = face[k % 2, pl.ds(tile * 8, 8), :]
                    t = jnp.where((here >= starts[r] - a) & (here < starts[r + 1] - a), shifted, t)
            avg_ref[pl.ds(a, 8), pl.ds(at, width)] = t

    bases = [0]
    for group in groups:
        bases.append(bases[-1] + (1 << len(group)))

    def spread(g, value):
        mine = bases[g] + rank(me, groups[g])
        red[mine] = value
        round_copies = [
            pltpu.make_async_remote_copy(
                src_ref=red.at[mine],
                dst_ref=red.at[mine],
                send_sem=sr_sem.at[bases[g] + which],
                recv_sem=rr_sem.at[bases[g] + which],
                device_id=(flips(me, groups[g], which),),
                device_id_type=MESH,
            )
            for which in range(1, 1 << len(groups[g]))
        ]
        for copy in round_copies:
            copy.start()
        return round_copies

    def gather(g, round_copies):
        for copy in round_copies:
            copy.wait_recv()
        total = red[bases[g]]
        for j in range(bases[g] + 1, bases[g + 1]):
            total = total + red[j]
        return total

    for ks in ((0, 1), (2, 3)):
        partial = partial + average(ks)
    partial = jnp.sum(partial, axis=0, keepdims=True)
    greeted(2)
    sends = spread(0, partial)
    issue(6)
    for k in range(HALF):
        place(k)
    average((4,))
    place(4)
    partial = gather(0, sends)
    last = spread(1, partial)
    sends += last
    issue(7)
    average((5,))
    place(5)
    average((6,))
    place(6)
    average((7,))
    place(7)
    partial = gather(1, last)
    inner_ref[0, 0] = jnp.sum(partial)

    for copy in sends:
        copy.wait_send()
    for copy in block_copies:
        copy.wait_send()
    for row in copies:
        for copy in row:
            copy.wait_send()


def copy_out(schur_ref, avg_ref, inner_ref, schur_out, avg_out, inner_out, sem):
    copies = [
        pltpu.make_async_copy(avg_ref, avg_out, sem.at[0]),
        pltpu.make_async_copy(schur_ref, schur_out, sem.at[1]),
    ]
    for copy in copies:
        copy.start()
    inner_out[0, 0] = inner_ref[0, 0]
    for copy in copies:
        copy.wait()


def local(inv_interior, coupling, boundary, residual, face_size, init_scale):
    ni, nb = coupling.shape
    columns = residual.shape[1]
    faces = face_size.shape[1]
    subs = lax.axis_size("sub")
    masks = [subs >> (r + 1) for r in range(faces)]
    groups = [[1, 2, 4], [8, 16, 32, 64]]
    slots = sum(1 << len(g) for g in groups)
    width = columns // CHUNKS
    f32, bf16 = jnp.float32, jnp.bfloat16
    anyspec = pl.BlockSpec(memory_space=pl.ANY)
    smem = pl.BlockSpec(memory_space=pltpu.SMEM)
    vmem = pl.BlockSpec(memory_space=pltpu.VMEM)
    dma = pltpu.SemaphoreType.DMA
    schur, averaged, inner = pl.pallas_call(
        functools.partial(kernel, masks, groups),
        name="deluxe",
        out_shape=(
            pltpu.VMEM((nb, nb), f32),
            pltpu.VMEM((nb, columns), f32),
            pltpu.SMEM((1, 1), f32),
        ),
        in_specs=[anyspec, anyspec, anyspec, anyspec, smem, smem],
        out_specs=(vmem, vmem, smem),
        scratch_shapes=[
            pltpu.VMEM((ni, ni), bf16),
            pltpu.VMEM((ni, nb), bf16),
            pltpu.VMEM((ni, nb), bf16),
            pltpu.VMEM((nb, nb), f32),
            pltpu.VMEM((nb, columns), f32),
            pltpu.VMEM((CHUNKS, faces, FMAX, width), f32),
            pltpu.VMEM((CHUNKS, faces, FMAX, width), f32),
            pltpu.VMEM((faces, FMAX, FMAX), f32),
            pltpu.VMEM((faces, FMAX, FMAX), f32),
            pltpu.VMEM((CHUNKS, faces, FMAX, width), f32),
            pltpu.VMEM((2, faces * SPAN + (faces - 1) * (FMAX // 2) - 8, width), f32),
            pltpu.VMEM((faces, 2 * FMAX, 2 * FMAX), bf16),
            pltpu.VMEM((slots, 1, 128), f32),
            dma((3,)),
            dma((ni // MROWS,)),
            dma((CHUNKS, faces)),
            dma((CHUNKS, faces)),
            dma((faces,)),
            dma((faces,)),
            dma((slots,)),
            dma((slots,)),
            pltpu.SemaphoreType.REGULAR((3,)),
        ],
        compiler_params=pltpu.CompilerParams(
            collective_id=0, has_side_effects=True, vmem_limit_bytes=56 * 2**20
        ),
    )(inv_interior, coupling, boundary, residual, face_size, init_scale)
    schur, averaged, inner = pl.pallas_call(
        copy_out,
        name="copy_out",
        out_shape=(
            jax.ShapeDtypeStruct((nb, nb), f32),
            jax.ShapeDtypeStruct((nb, columns), f32),
            jax.ShapeDtypeStruct((1, 1), f32),
        ),
        in_specs=[vmem, vmem, smem],
        out_specs=(anyspec, anyspec, smem),
        scratch_shapes=[dma((2,))],
    )(
        pltpu.with_memory_space_constraint(schur, pltpu.VMEM),
        pltpu.with_memory_space_constraint(averaged, pltpu.VMEM),
        pltpu.with_memory_space_constraint(inner, pltpu.SMEM),
    )
    return (schur, averaged, inner[0, 0])


def solution(mesh):
    spec = P("sub", None)
    return jax.shard_map(
        local,
        mesh=mesh,
        in_specs=(spec,) * 6,
        out_specs=(spec, spec, P()),
        check_vma=False,
    )
```

```python
import functools

import jax
import jax.numpy as jnp
from jax import lax
from jax.experimental import pallas as pl
from jax.experimental.pallas import tpu as pltpu
from jax.sharding import PartitionSpec as P

FMAX = 128
STEPS = 4
CHUNKS = 8
EARLY = 3
HALF = CHUNKS // 2
MROWS = 512
SPAN = FMAX + 8
MESH = pl.DeviceIdType.MESH


def flip(me, mask):
    return me + mask - 2 * mask * ((me // mask) % 2)


def flips(me, masks, which):
    for bit, mask in enumerate(masks):
        if (which >> bit) & 1:
            me = flip(me, mask)
    return me


def rank(me, masks):
    total = 0
    for bit, mask in enumerate(masks):
        total = total + ((me // mask) % 2) * (1 << bit)
    return total


def halves(x):
    hi = x.astype(jnp.bfloat16)
    lo = (x - hi.astype(jnp.float32)).astype(jnp.bfloat16)
    return hi, lo


def mm(a, b):
    return jnp.dot(a, b, preferred_element_type=jnp.float32)


def square_product(a, b):
    ah, al = halves(a)
    bh, bl = halves(b)
    row = jnp.concatenate([bh, bl], axis=1)
    both = mm(jnp.concatenate([ah, al], axis=1), jnp.concatenate([row, row], axis=0))
    return both[:, :FMAX] + both[:, FMAX:]


def turned(x, shift):
    amount = jnp.full((1, 8, x.shape[2]), shift, jnp.int32)
    for bit in (1, 2, 4):
        x = jnp.where((amount & bit) != 0, jnp.roll(x, bit, axis=1), x)
    return x


def rows_at(ref, start, columns):
    base = jnp.minimum(lax.div(start, 8), (ref.shape[0] - FMAX) // 8 - 1) * 8
    shift = start - base
    x = ref[pl.ds(base, FMAX + 8), columns]
    w = x.shape[1]
    x = turned(x.reshape(FMAX // 8 + 1, 8, w), 8 - shift)
    row = lax.broadcasted_iota(jnp.int32, (1, 8, w), 1)
    return jnp.where(row < 8 - shift, x[:-1], x[1:]).reshape(FMAX, w)


def rows_down(x, shift):
    w = x.shape[1]
    pad = jnp.zeros((1, 8, w), x.dtype)
    x = jnp.concatenate([pad, x.reshape(FMAX // 8, 8, w), pad], axis=0)
    x = turned(x, shift)
    row = lax.broadcasted_iota(jnp.int32, (1, 8, w), 1)
    return jnp.where(row < shift, x[:-1], x[1:]).reshape(FMAX + 8, w)


def kernel(
    masks,
    groups,
    inv_hbm,
    cpl_hbm,
    bnd_hbm,
    res_hbm,
    size_hbm,
    scale_hbm,
    schur_ref,
    avg_ref,
    inner_ref,
    size_ref,
    scale_ref,
    small_sem,
    inv,
    cpl,
    sol,
    bnd,
    res,
    own,
    oth,
    own_b,
    oth_b,
    val,
    face,
    wbuf,
    red,
    in_sem,
    inv_sem,
    s_sem,
    r_sem,
    sb_sem,
    rb_sem,
    sr_sem,
    rr_sem,
    hello_sem,
):
    me = lax.axis_index("sub")
    faces = len(masks)
    ni, nb = cpl.shape
    columns = res.shape[1]
    width = columns // CHUNKS

    mates = [flip(me, mask) for mask in masks]
    peers = [flip(me, mask) for group in groups for mask in group]
    barrier = pltpu.get_barrier_semaphore()
    for peer in peers:
        pl.semaphore_signal(barrier, inc=1, device_id=(peer,), device_id_type=MESH)

    load_size = pltpu.make_async_copy(size_hbm, size_ref, small_sem.at[0])
    load_size.start()
    load_scale = pltpu.make_async_copy(scale_hbm, scale_ref, small_sem.at[1])
    load_scale.start()
    odd = 0
    for mask in masks:
        odd = odd + (me // mask) % 2
    odd = odd % 2

    def column(k):
        return pl.multiple_of(((1 - odd) * k + odd * (CHUNKS - 1 - k)) * width, width)

    load_res = pltpu.make_async_copy(res_hbm, res, in_sem.at[0])
    load_res.start()
    load_size.wait()
    load_scale.wait()
    sizes = [size_ref[0, r] for r in range(faces)]
    starts = [jnp.int32(0)]
    for r in range(faces):
        starts.append(starts[-1] + sizes[r])
    whole = [lax.div(start, 8) * 8 for start in starts]
    face[...] = jnp.zeros_like(face)

    copies = [
        [
            pltpu.make_async_remote_copy(
                src_ref=own.at[k, r],
                dst_ref=oth.at[k, r],
                send_sem=s_sem.at[k, r],
                recv_sem=r_sem.at[k, r],
                device_id=(mates[r],),
                device_id_type=MESH,
            )
            for r in range(faces)
        ]
        for k in range(CHUNKS)
    ]

    def issue(k, part=0):
        for r in range(faces):
            if part == 0 or r % 2 == part - 1:
                copies[k][r].start()

    rows = lax.broadcasted_iota(jnp.int32, (FMAX, width), 0)

    def greet(stage):
        for peer in peers:
            pl.semaphore_signal(
                hello_sem.at[stage], inc=1, device_id=(peer,), device_id_type=MESH
            )

    def greeted(stage):
        pl.semaphore_wait(hello_sem.at[stage], len(peers))

    def extract(k):
        for r in range(faces):
            piece = rows_at(res, starts[r], pl.ds(column(k), width))
            own[k, r] = jnp.where(rows < sizes[r], piece, 0.0)

    load_res.wait()
    extract(0)
    load_cpl = pltpu.make_async_copy(cpl_hbm, cpl, in_sem.at[1])
    load_cpl.start()
    load_inv = [
        pltpu.make_async_copy(
            inv_hbm.at[pl.ds(i * MROWS, MROWS)], inv.at[pl.ds(i * MROWS, MROWS)], inv_sem.at[i]
        )
        for i in range(ni // MROWS)
    ]
    for copy in load_inv:
        copy.start()
    load_bnd = pltpu.make_async_copy(bnd_hbm, bnd, in_sem.at[2])
    load_bnd.start()
    pl.semaphore_wait(barrier, len(peers))
    issue(0)
    extract(1)
    greet(0)
    load_cpl.wait()
    steps = ni // MROWS
    for i in range(steps):
        load_inv[i].wait()
        if i + 2 < CHUNKS:
            extract(i + 2)
        sol[pl.ds(i * MROWS, MROWS), :] = mm(inv[pl.ds(i * MROWS, MROWS), :], cpl[...]).astype(
            jnp.bfloat16
        )
        if i + 1 < EARLY:
            issue(i + 1)
    for k in range(steps + 2, CHUNKS):
        extract(k)
    greeted(0)
    greet(1)
    load_bnd.wait()
    schur_ref[...] = bnd[...] - lax.dot_general(
        cpl[...], sol[...], (((0,), (0,)), ((), ())), preferred_element_type=jnp.float32
    )

    i0 = lax.broadcasted_iota(jnp.int32, (FMAX, FMAX), 0)
    i1 = lax.broadcasted_iota(jnp.int32, (FMAX, FMAX), 1)
    block_copies = [
        pltpu.make_async_remote_copy(
            src_ref=own_b.at[r],
            dst_ref=oth_b.at[r],
            send_sem=sb_sem.at[r],
            recv_sem=rb_sem.at[r],
            device_id=(mates[r],),
            device_id_type=MESH,
        )
        for r in range(faces)
    ]
    for r in range(faces):
        left = jnp.minimum(lax.div(starts[r], FMAX), nb // FMAX - 2) * FMAX
        band = rows_at(schur_ref, starts[r], pl.ds(left, 2 * FMAX))
        b0 = lax.broadcasted_iota(jnp.int32, (2 * FMAX, FMAX), 0)
        b1 = lax.broadcasted_iota(jnp.int32, (2 * FMAX, FMAX), 1)
        pick = jnp.where(b0 == b1 + (starts[r] - left), 1.0, 0.0).astype(jnp.bfloat16)
        hi, lo = halves(band)
        rest = band - hi.astype(jnp.float32) - lo.astype(jnp.float32)
        parts = mm(jnp.concatenate([hi, lo, rest.astype(jnp.bfloat16)], axis=0), pick)
        block = parts[:FMAX] + parts[FMAX : 2 * FMAX] + parts[2 * FMAX :]
        own_b[r] = jnp.where((i0 < sizes[r]) & (i1 < sizes[r]), block, 0.0)
        if r > 0:
            block_copies[r - 1].start()
    block_copies[faces - 1].start()
    for k in range(EARLY, HALF + 2):
        issue(k)
    greeted(1)
    greet(2)

    es, xs = [], []
    for r in range(faces):
        block_copies[r].wait_recv()
        scale = scale_ref[0, r]
        ident = jnp.where((i0 == i1) & (i0 < sizes[r]), 1.0, 0.0)
        e = ident - scale * (own_b[r] + oth_b[r])
        xs.append(scale * (ident + e))
        es.append(e)
    for step in range(1, STEPS):
        es = [square_product(e, e) for e in es]
        xs = [x + square_product(x, e) for x, e in zip(xs, es)]
    for r in range(faces):
        w = jnp.concatenate(
            [square_product(xs[r], own_b[r]), square_product(xs[r], oth_b[r])], axis=1
        )
        wh, wl = halves(w)
        wbuf[r, pl.ds(0, FMAX), :] = wh
        wbuf[r, pl.ds(FMAX, FMAX), :] = wl

    def fold(x):
        total = None
        for a in range(0, x.shape[0], 8):
            for b in range(0, x.shape[1], 128):
                t = x[a : a + 8, b : b + 128]
                total = t if total is None else total + t
        return total

    row8 = lax.broadcasted_iota(jnp.int32, (8, 128), 0)
    partial = jnp.zeros((8, 128), jnp.float32)
    low = faces * (FMAX // 2)
    for a in range(low, nb, 8):
        t = res[pl.ds(a, 8), :]
        t = fold(t * t)
        partial = partial + jnp.where(row8 + a >= starts[faces], t, 0.0)

    def average(ks):
        pair = jnp.zeros((8, 128), jnp.float32)
        for r in range(faces):
            for k in ks:
                copies[k][r].wait_recv()
            both = [jnp.concatenate([own[CHUNKS - 1 - k, r], oth[k, r]], axis=0) for k in ks]
            ph, pw = halves(jnp.concatenate(both, axis=1))
            top = mm(wbuf[r], ph)
            value = top[:FMAX] + top[FMAX:] + mm(wbuf[r, pl.ds(0, FMAX), :], pw)
            for j, k in enumerate(ks):
                part = value[:, j * width : (j + 1) * width]
                val[k, r] = part
                if k < HALF:
                    pair = pair + fold((both[j][:FMAX] + both[j][FMAX:]) * part)
        return pair

    def place(k):
        at = column(CHUNKS - 1 - k)
        for r in range(faces):
            face[k % 2, pl.ds(r * SPAN, SPAN), :] = rows_down(val[k, r], starts[r] - whole[r])
        here = lax.broadcasted_iota(jnp.int32, (8, width), 0)
        for a in range(0, nb, 8):
            t = res[pl.ds(a, 8), pl.ds(at, width)]
            for r in range(faces):
                if a >= r * (FMAX // 2) and a < (r + 1) * FMAX:
                    tile = a // 8 + r * (SPAN // 8) - lax.div(starts[r], 8)
                    tile = jnp.clip(tile, 0, face.shape[1] // 8 - 1)
                    shifted = face[k % 2, pl.ds(tile * 8, 8), :]
                    t = jnp.where((here >= starts[r] - a) & (here < starts[r + 1] - a), shifted, t)
            avg_ref[pl.ds(a, 8), pl.ds(at, width)] = t

    bases = [0]
    for group in groups:
        bases.append(bases[-1] + (1 << len(group)))

    def spread(g, value):
        mine = bases[g] + rank(me, groups[g])
        red[mine] = value
        round_copies = [
            pltpu.make_async_remote_copy(
                src_ref=red.at[mine],
                dst_ref=red.at[mine],
                send_sem=sr_sem.at[bases[g] + which],
                recv_sem=rr_sem.at[bases[g] + which],
                device_id=(flips(me, groups[g], which),),
                device_id_type=MESH,
            )
            for which in range(1, 1 << len(groups[g]))
        ]
        for copy in round_copies:
            copy.start()
        return round_copies

    def gather(g, round_copies):
        for copy in round_copies:
            copy.wait_recv()
        total = red[bases[g]]
        for j in range(bases[g] + 1, bases[g + 1]):
            total = total + red[j]
        return total

    for ks in ((0, 1), (2, 3)):
        partial = partial + average(ks)
    partial = jnp.sum(partial, axis=0, keepdims=True)
    greeted(2)
    sends = spread(0, partial)
    issue(6)
    for k in range(HALF):
        place(k)
    average((4,))
    place(4)
    partial = gather(0, sends)
    last = spread(1, partial)
    sends += last
    issue(7)
    average((5,))
    place(5)
    average((6,))
    place(6)
    average((7,))
    place(7)
    partial = gather(1, last)
    inner_ref[0, 0] = jnp.sum(partial)

    for copy in sends:
        copy.wait_send()
    for copy in block_copies:
        copy.wait_send()
    for row in copies:
        for copy in row:
            copy.wait_send()


def copy_out(schur_ref, avg_ref, inner_ref, schur_out, avg_out, inner_out, sem):
    copies = [
        pltpu.make_async_copy(avg_ref, avg_out, sem.at[0]),
        pltpu.make_async_copy(schur_ref, schur_out, sem.at[1]),
        pltpu.make_async_copy(inner_ref, inner_out, sem.at[2]),
    ]
    for copy in copies:
        copy.start()
    for copy in copies:
        copy.wait()


def local(inv_interior, coupling, boundary, residual, face_size, init_scale):
    ni, nb = coupling.shape
    columns = residual.shape[1]
    faces = face_size.shape[1]
    subs = lax.axis_size("sub")
    masks = [subs >> (r + 1) for r in range(faces)]
    groups = [[1, 2, 4], [8, 16, 32, 64]]
    slots = sum(1 << len(g) for g in groups)
    width = columns // CHUNKS
    f32, bf16 = jnp.float32, jnp.bfloat16
    anyspec = pl.BlockSpec(memory_space=pl.ANY)
    smem = pl.BlockSpec(memory_space=pltpu.SMEM)
    vmem = pl.BlockSpec(memory_space=pltpu.VMEM)
    dma = pltpu.SemaphoreType.DMA
    schur, averaged, inner = pl.pallas_call(
        functools.partial(kernel, masks, groups),
        name="deluxe",
        out_shape=(
            pltpu.VMEM((nb, nb), f32),
            pltpu.VMEM((nb, columns), f32),
            pltpu.SMEM((1, 1), f32),
        ),
        in_specs=[anyspec] * 6,
        out_specs=(vmem, vmem, smem),
        scratch_shapes=[
            pltpu.SMEM((1, faces), jnp.int32),
            pltpu.SMEM((1, faces), f32),
            dma((2,)),
            pltpu.VMEM((ni, ni), bf16),
            pltpu.VMEM((ni, nb), bf16),
            pltpu.VMEM((ni, nb), bf16),
            pltpu.VMEM((nb, nb), f32),
            pltpu.VMEM((nb, columns), f32),
            pltpu.VMEM((CHUNKS, faces, FMAX, width), f32),
            pltpu.VMEM((CHUNKS, faces, FMAX, width), f32),
            pltpu.VMEM((faces, FMAX, FMAX), f32),
            pltpu.VMEM((faces, FMAX, FMAX), f32),
            pltpu.VMEM((CHUNKS, faces, FMAX, width), f32),
            pltpu.VMEM((2, faces * SPAN + (faces - 1) * (FMAX // 2) - 8, width), f32),
            pltpu.VMEM((faces, 2 * FMAX, 2 * FMAX), bf16),
            pltpu.VMEM((slots, 1, 128), f32),
            dma((3,)),
            dma((ni // MROWS,)),
            dma((CHUNKS, faces)),
            dma((CHUNKS, faces)),
            dma((faces,)),
            dma((faces,)),
            dma((slots,)),
            dma((slots,)),
            pltpu.SemaphoreType.REGULAR((3,)),
        ],
        compiler_params=pltpu.CompilerParams(
            collective_id=0, has_side_effects=True, vmem_limit_bytes=56 * 2**20
        ),
    )(inv_interior, coupling, boundary, residual, face_size, init_scale)
    schur, averaged, inner = pl.pallas_call(
        copy_out,
        name="copy_out",
        out_shape=(
            jax.ShapeDtypeStruct((nb, nb), f32),
            jax.ShapeDtypeStruct((nb, columns), f32),
            jax.ShapeDtypeStruct((1, 1), f32),
        ),
        in_specs=[vmem, vmem, smem],
        out_specs=(anyspec, anyspec, anyspec),
        scratch_shapes=[dma((3,))],
    )(
        pltpu.with_memory_space_constraint(schur, pltpu.VMEM),
        pltpu.with_memory_space_constraint(averaged, pltpu.VMEM),
        pltpu.with_memory_space_constraint(inner, pltpu.SMEM),
    )
    return (schur, averaged, inner[0, 0])


def solution(mesh):
    spec = P("sub", None)
    return jax.shard_map(
        local,
        mesh=mesh,
        in_specs=(spec,) * 6,
        out_specs=(spec, spec, P()),
        check_vma=False,
    )
```

```python
import functools

import jax
import jax.numpy as jnp
from jax import lax
from jax.experimental import pallas as pl
from jax.experimental.pallas import tpu as pltpu
from jax.sharding import PartitionSpec as P

FMAX = 128
STEPS = 4
CHUNKS = 8
EARLY = 3
HALF = CHUNKS // 2
MROWS = 512
SPAN = FMAX + 8
MESH = pl.DeviceIdType.MESH


def flip(me, mask):
    return me + mask - 2 * mask * ((me // mask) % 2)


def flips(me, masks, which):
    for bit, mask in enumerate(masks):
        if (which >> bit) & 1:
            me = flip(me, mask)
    return me


def rank(me, masks):
    total = 0
    for bit, mask in enumerate(masks):
        total = total + ((me // mask) % 2) * (1 << bit)
    return total


def halves(x):
    hi = x.astype(jnp.bfloat16)
    lo = (x - hi.astype(jnp.float32)).astype(jnp.bfloat16)
    return hi, lo


def mm(a, b):
    return jnp.dot(a, b, preferred_element_type=jnp.float32)


def square_product(a, b):
    ah, al = halves(a)
    bh, bl = halves(b)
    row = jnp.concatenate([bh, bl], axis=1)
    both = mm(jnp.concatenate([ah, al], axis=1), jnp.concatenate([row, row], axis=0))
    return both[:, :FMAX] + both[:, FMAX:]


def turned(x, shift):
    amount = jnp.full((1, 8, x.shape[2]), shift, jnp.int32)
    for bit in (1, 2, 4):
        x = jnp.where((amount & bit) != 0, jnp.roll(x, bit, axis=1), x)
    return x


def rows_at(ref, start, columns):
    base = jnp.minimum(lax.div(start, 8), (ref.shape[0] - FMAX) // 8 - 1) * 8
    shift = start - base
    x = ref[pl.ds(base, FMAX + 8), columns]
    w = x.shape[1]
    x = turned(x.reshape(FMAX // 8 + 1, 8, w), 8 - shift)
    row = lax.broadcasted_iota(jnp.int32, (1, 8, w), 1)
    return jnp.where(row < 8 - shift, x[:-1], x[1:]).reshape(FMAX, w)


def rows_down(x, shift):
    w = x.shape[1]
    pad = jnp.zeros((1, 8, w), x.dtype)
    x = jnp.concatenate([pad, x.reshape(FMAX // 8, 8, w), pad], axis=0)
    x = turned(x, shift)
    row = lax.broadcasted_iota(jnp.int32, (1, 8, w), 1)
    return jnp.where(row < shift, x[:-1], x[1:]).reshape(FMAX + 8, w)


def kernel(
    masks,
    groups,
    inv_hbm,
    cpl_hbm,
    bnd_hbm,
    res_hbm,
    size_hbm,
    scale_hbm,
    schur_ref,
    avg_ref,
    inner_ref,
    size_ref,
    scale_ref,
    small_sem,
    inv,
    cpl,
    sol,
    bnd,
    res,
    own,
    oth,
    own_b,
    oth_b,
    val,
    face,
    wbuf,
    red,
    in_sem,
    inv_sem,
    s_sem,
    r_sem,
    sb_sem,
    rb_sem,
    sr_sem,
    rr_sem,
    hello_sem,
):
    me = lax.axis_index("sub")
    faces = len(masks)
    ni, nb = cpl.shape
    columns = res.shape[1]
    width = columns // CHUNKS

    mates = [flip(me, mask) for mask in masks]
    peers = [flip(me, mask) for group in groups for mask in group]
    barrier = pltpu.get_barrier_semaphore()
    for peer in peers:
        pl.semaphore_signal(barrier, inc=1, device_id=(peer,), device_id_type=MESH)

    load_size = pltpu.make_async_copy(size_hbm, size_ref, small_sem.at[0])
    load_size.start()
    load_scale = pltpu.make_async_copy(scale_hbm, scale_ref, small_sem.at[1])
    load_scale.start()
    odd = 0
    for mask in masks:
        odd = odd + (me // mask) % 2
    odd = odd % 2

    def column(k):
        return pl.multiple_of(((1 - odd) * k + odd * (CHUNKS - 1 - k)) * width, width)

    load_res = pltpu.make_async_copy(res_hbm, res, in_sem.at[0])
    load_res.start()
    load_size.wait()
    load_scale.wait()
    sizes = [size_ref[0, r] for r in range(faces)]
    starts = [jnp.int32(0)]
    for r in range(faces):
        starts.append(starts[-1] + sizes[r])
    whole = [lax.div(start, 8) * 8 for start in starts]

    copies = [
        [
            pltpu.make_async_remote_copy(
                src_ref=own.at[k, r],
                dst_ref=oth.at[k, r],
                send_sem=s_sem.at[k, r],
                recv_sem=r_sem.at[k, r],
                device_id=(mates[r],),
                device_id_type=MESH,
            )
            for r in range(faces)
        ]
        for k in range(CHUNKS)
    ]

    def issue(k, part=0):
        for r in range(faces):
            if part == 0 or r % 2 == part - 1:
                copies[k][r].start()

    rows = lax.broadcasted_iota(jnp.int32, (FMAX, width), 0)

    def greet(stage):
        for peer in peers:
            pl.semaphore_signal(
                hello_sem.at[stage], inc=1, device_id=(peer,), device_id_type=MESH
            )

    def greeted(stage):
        pl.semaphore_wait(hello_sem.at[stage], len(peers))

    def extract(k):
        for r in range(faces):
            piece = rows_at(res, starts[r], pl.ds(column(k), width))
            own[k, r] = jnp.where(rows < sizes[r], piece, 0.0)

    load_res.wait()
    extract(0)
    load_cpl = pltpu.make_async_copy(cpl_hbm, cpl, in_sem.at[1])
    load_cpl.start()
    load_inv = [
        pltpu.make_async_copy(
            inv_hbm.at[pl.ds(i * MROWS, MROWS)], inv.at[pl.ds(i * MROWS, MROWS)], inv_sem.at[i]
        )
        for i in range(ni // MROWS)
    ]
    for copy in load_inv:
        copy.start()
    load_bnd = pltpu.make_async_copy(bnd_hbm, bnd, in_sem.at[2])
    load_bnd.start()
    pl.semaphore_wait(barrier, len(peers))
    issue(0)
    extract(1)
    face[...] = jnp.zeros_like(face)
    greet(0)
    load_cpl.wait()
    steps = ni // MROWS
    for i in range(steps):
        load_inv[i].wait()
        if i + 2 <= EARLY:
            extract(i + 2)
        sol[pl.ds(i * MROWS, MROWS), :] = mm(inv[pl.ds(i * MROWS, MROWS), :], cpl[...]).astype(
            jnp.bfloat16
        )
        if i + 1 < EARLY:
            issue(i + 1)
    greeted(0)
    greet(1)
    load_bnd.wait()
    schur_ref[...] = bnd[...] - lax.dot_general(
        cpl[...], sol[...], (((0,), (0,)), ((), ())), preferred_element_type=jnp.float32
    )

    i0 = lax.broadcasted_iota(jnp.int32, (FMAX, FMAX), 0)
    i1 = lax.broadcasted_iota(jnp.int32, (FMAX, FMAX), 1)
    block_copies = [
        pltpu.make_async_remote_copy(
            src_ref=own_b.at[r],
            dst_ref=oth_b.at[r],
            send_sem=sb_sem.at[r],
            recv_sem=rb_sem.at[r],
            device_id=(mates[r],),
            device_id_type=MESH,
        )
        for r in range(faces)
    ]
    for r in range(faces):
        left = jnp.minimum(lax.div(starts[r], FMAX), nb // FMAX - 2) * FMAX
        band = rows_at(schur_ref, starts[r], pl.ds(left, 2 * FMAX))
        b0 = lax.broadcasted_iota(jnp.int32, (2 * FMAX, FMAX), 0)
        b1 = lax.broadcasted_iota(jnp.int32, (2 * FMAX, FMAX), 1)
        pick = jnp.where(b0 == b1 + (starts[r] - left), 1.0, 0.0).astype(jnp.bfloat16)
        hi, lo = halves(band)
        rest = band - hi.astype(jnp.float32) - lo.astype(jnp.float32)
        parts = mm(jnp.concatenate([hi, lo, rest.astype(jnp.bfloat16)], axis=0), pick)
        block = parts[:FMAX] + parts[FMAX : 2 * FMAX] + parts[2 * FMAX :]
        own_b[r] = jnp.where((i0 < sizes[r]) & (i1 < sizes[r]), block, 0.0)
        if r > 0:
            block_copies[r - 1].start()
    block_copies[faces - 1].start()
    issue(EARLY)
    for k in range(EARLY + 1, CHUNKS):
        extract(k)
        if EARLY + 1 < k <= HALF + 2:
            issue(k - 1)
    greeted(1)
    greet(2)

    es, xs = [], []
    for r in range(faces):
        block_copies[r].wait_recv()
        scale = scale_ref[0, r]
        ident = jnp.where((i0 == i1) & (i0 < sizes[r]), 1.0, 0.0)
        e = ident - scale * (own_b[r] + oth_b[r])
        xs.append(scale * (ident + e))
        es.append(e)
    for step in range(1, STEPS):
        es = [square_product(e, e) for e in es]
        xs = [x + square_product(x, e) for x, e in zip(xs, es)]
    for r in range(faces):
        w = jnp.concatenate(
            [square_product(xs[r], own_b[r]), square_product(xs[r], oth_b[r])], axis=1
        )
        wh, wl = halves(w)
        wbuf[r, pl.ds(0, FMAX), :] = wh
        wbuf[r, pl.ds(FMAX, FMAX), :] = wl

    def fold(x):
        total = None
        for a in range(0, x.shape[0], 8):
            for b in range(0, x.shape[1], 128):
                t = x[a : a + 8, b : b + 128]
                total = t if total is None else total + t
        return total

    row8 = lax.broadcasted_iota(jnp.int32, (8, 128), 0)
    partial = jnp.zeros((8, 128), jnp.float32)
    low = faces * (FMAX // 2)
    for a in range(low, nb, 8):
        t = res[pl.ds(a, 8), :]
        t = fold(t * t)
        partial = partial + jnp.where(row8 + a >= starts[faces], t, 0.0)

    def average(ks):
        pair = jnp.zeros((8, 128), jnp.float32)
        for r in range(faces):
            for k in ks:
                copies[k][r].wait_recv()
            both = [jnp.concatenate([own[CHUNKS - 1 - k, r], oth[k, r]], axis=0) for k in ks]
            ph, pw = halves(jnp.concatenate(both, axis=1))
            top = mm(wbuf[r], ph)
            value = top[:FMAX] + top[FMAX:] + mm(wbuf[r, pl.ds(0, FMAX), :], pw)
            for j, k in enumerate(ks):
                part = value[:, j * width : (j + 1) * width]
                val[k, r] = part
                if k < HALF:
                    pair = pair + fold((both[j][:FMAX] + both[j][FMAX:]) * part)
        return pair

    def place(k):
        at = column(CHUNKS - 1 - k)
        for r in range(faces):
            face[k % 2, pl.ds(r * SPAN, SPAN), :] = rows_down(val[k, r], starts[r] - whole[r])
        here = lax.broadcasted_iota(jnp.int32, (8, width), 0)
        for a in range(0, nb, 8):
            t = res[pl.ds(a, 8), pl.ds(at, width)]
            for r in range(faces):
                if a >= r * (FMAX // 2) and a < (r + 1) * FMAX:
                    tile = a // 8 + r * (SPAN // 8) - lax.div(starts[r], 8)
                    tile = jnp.clip(tile, 0, face.shape[1] // 8 - 1)
                    shifted = face[k % 2, pl.ds(tile * 8, 8), :]
                    t = jnp.where((here >= starts[r] - a) & (here < starts[r + 1] - a), shifted, t)
            avg_ref[pl.ds(a, 8), pl.ds(at, width)] = t

    bases = [0]
    for group in groups:
        bases.append(bases[-1] + (1 << len(group)))

    def spread(g, value):
        mine = bases[g] + rank(me, groups[g])
        red[mine] = value
        round_copies = [
            pltpu.make_async_remote_copy(
                src_ref=red.at[mine],
                dst_ref=red.at[mine],
                send_sem=sr_sem.at[bases[g] + which],
                recv_sem=rr_sem.at[bases[g] + which],
                device_id=(flips(me, groups[g], which),),
                device_id_type=MESH,
            )
            for which in range(1, 1 << len(groups[g]))
        ]
        for copy in round_copies:
            copy.start()
        return round_copies

    def gather(g, round_copies):
        for copy in round_copies:
            copy.wait_recv()
        total = red[bases[g]]
        for j in range(bases[g] + 1, bases[g + 1]):
            total = total + red[j]
        return total

    for ks in ((0, 1), (2, 3)):
        partial = partial + average(ks)
    partial = jnp.sum(partial, axis=0, keepdims=True)
    greeted(2)
    sends = spread(0, partial)
    issue(6)
    for k in range(HALF):
        place(k)
    average((4,))
    place(4)
    partial = gather(0, sends)
    last = spread(1, partial)
    sends += last
    issue(7)
    average((5,))
    place(5)
    average((6,))
    place(6)
    average((7,))
    place(7)
    partial = gather(1, last)
    inner_ref[0, 0] = jnp.sum(partial)

    for copy in sends:
        copy.wait_send()
    for copy in block_copies:
        copy.wait_send()
    for row in copies:
        for copy in row:
            copy.wait_send()


def copy_out(schur_ref, avg_ref, inner_ref, schur_out, avg_out, inner_out, sem):
    copies = [
        pltpu.make_async_copy(avg_ref, avg_out, sem.at[0]),
        pltpu.make_async_copy(schur_ref, schur_out, sem.at[1]),
        pltpu.make_async_copy(inner_ref, inner_out, sem.at[2]),
    ]
    for copy in copies:
        copy.start()
    for copy in copies:
        copy.wait()


def local(inv_interior, coupling, boundary, residual, face_size, init_scale):
    ni, nb = coupling.shape
    columns = residual.shape[1]
    faces = face_size.shape[1]
    subs = lax.axis_size("sub")
    masks = [subs >> (r + 1) for r in range(faces)]
    groups = [[1, 2, 4], [8, 16, 32, 64]]
    slots = sum(1 << len(g) for g in groups)
    width = columns // CHUNKS
    f32, bf16 = jnp.float32, jnp.bfloat16
    anyspec = pl.BlockSpec(memory_space=pl.ANY)
    smem = pl.BlockSpec(memory_space=pltpu.SMEM)
    vmem = pl.BlockSpec(memory_space=pltpu.VMEM)
    dma = pltpu.SemaphoreType.DMA
    schur, averaged, inner = pl.pallas_call(
        functools.partial(kernel, masks, groups),
        name="deluxe",
        out_shape=(
            pltpu.VMEM((nb, nb), f32),
            pltpu.VMEM((nb, columns), f32),
            pltpu.SMEM((1, 1), f32),
        ),
        in_specs=[anyspec] * 6,
        out_specs=(vmem, vmem, smem),
        scratch_shapes=[
            pltpu.SMEM((1, faces), jnp.int32),
            pltpu.SMEM((1, faces), f32),
            dma((2,)),
            pltpu.VMEM((ni, ni), bf16),
            pltpu.VMEM((ni, nb), bf16),
            pltpu.VMEM((ni, nb), bf16),
            pltpu.VMEM((nb, nb), f32),
            pltpu.VMEM((nb, columns), f32),
            pltpu.VMEM((CHUNKS, faces, FMAX, width), f32),
            pltpu.VMEM((CHUNKS, faces, FMAX, width), f32),
            pltpu.VMEM((faces, FMAX, FMAX), f32),
            pltpu.VMEM((faces, FMAX, FMAX), f32),
            pltpu.VMEM((CHUNKS, faces, FMAX, width), f32),
            pltpu.VMEM((2, faces * SPAN + (faces - 1) * (FMAX // 2) - 8, width), f32),
            pltpu.VMEM((faces, 2 * FMAX, 2 * FMAX), bf16),
            pltpu.VMEM((slots, 1, 128), f32),
            dma((3,)),
            dma((ni // MROWS,)),
            dma((CHUNKS, faces)),
            dma((CHUNKS, faces)),
            dma((faces,)),
            dma((faces,)),
            dma((slots,)),
            dma((slots,)),
            pltpu.SemaphoreType.REGULAR((3,)),
        ],
        compiler_params=pltpu.CompilerParams(
            collective_id=0, has_side_effects=True, vmem_limit_bytes=56 * 2**20
        ),
    )(inv_interior, coupling, boundary, residual, face_size, init_scale)
    schur, averaged, inner = pl.pallas_call(
        copy_out,
        name="copy_out",
        out_shape=(
            jax.ShapeDtypeStruct((nb, nb), f32),
            jax.ShapeDtypeStruct((nb, columns), f32),
            jax.ShapeDtypeStruct((1, 1), f32),
        ),
        in_specs=[vmem, vmem, smem],
        out_specs=(anyspec, anyspec, anyspec),
        scratch_shapes=[dma((3,))],
    )(
        pltpu.with_memory_space_constraint(schur, pltpu.VMEM),
        pltpu.with_memory_space_constraint(averaged, pltpu.VMEM),
        pltpu.with_memory_space_constraint(inner, pltpu.SMEM),
    )
    return (schur, averaged, inner[0, 0])


def solution(mesh):
    spec = P("sub", None)
    return jax.shard_map(
        local,
        mesh=mesh,
        in_specs=(spec,) * 6,
        out_specs=(spec, spec, P()),
        check_vma=False,
    )
```
